256 devices in a mesh: species: 16 (over y, z_lo, core), tile: 16 (over x, z_hi).
Axes of the slice: x: 4, y: 4, z: 8 (z_hi: 4, z_lo: 2; z = z_hi * 2 + z_lo), core: 2. Of those that a mesh axis runs over, the one named last changes fastest.
Arguments:
- tracers: float32 [256, 16, 128, 128], P('species', None, 'tile'), may hold values from 0.1 to 4
- fluxes: float32 [4, 3, 16, 128, 128], P(None, None, 'species', 'tile'), may hold values from -0.15 to 0.15
- weight_in: bfloat16 [512, 256], replicated, may hold values from -0.375 to 0.375
- weight_out: bfloat16 [256, 512], replicated, may hold values from -0.25 to 0.25
Outputs:
- tracers_out: float32 [256, 16, 128, 128], P('species', None, 'tile')
The draws below stay inside these ranges and needn't reach their ends.
All inputs are finite; a program needn't handle non-finite values.
Results may differ from the reference program's by a relative error of at most 0.0035.
Values may be sent and summed in bfloat16 or wider, within the bound.
A program may use at most 64 MiB of HBM per device.

```python
import math
from functools import partial
import jax
import jax.numpy as jnp
from jax import lax

SPECIES = 256
HID = 512
NZ = 16
NY = 128
STEPS = 4
NX = 128


def level_of(own_key, dims, split, least, largest):
    factor_of, own = 1.0, jax.random.fold_in(own_key, 6)
    for dim, parts in split:
        steps = jnp.exp(jax.random.uniform(jax.random.fold_in(own, dim), (parts,), jnp.float32, least / len(split), largest / len(split)))
        factor_of = factor_of * jnp.repeat(steps, dims[dim] // parts).reshape([-1 if axis == dim else 1 for axis in range(len(dims))])
    return factor_of


def bell_draw(stream_key, dims, deviation, limit, dtype=jnp.bfloat16):
    result = jax.random.normal(stream_key, dims, jnp.float32) * deviation
    return jnp.minimum(jnp.maximum(result, -limit), limit).astype(dtype)


def setup_inputs(seed: int = 0) -> dict:
    seeds = jax.random.split(jax.random.key(seed), 5)
    tracers = jnp.clip(jnp.exp(math.log(4.0) - 3.6888794 * jax.random.uniform(seeds[0], (SPECIES, NZ, NX, NY), jnp.float32) ** level_of(seeds[0], (SPECIES, NZ, NX, NY), ((0, 16), (2, 16)), -0.2, 0.2)), 0.1, 4.0)
    fluxes = jnp.clip(jax.random.uniform(seeds[1], (STEPS, 3, NZ, NX, NY), jnp.float32, -0.15, 0.15) * level_of(seeds[1], (STEPS, 3, NZ, NX, NY), ((2, 16), (3, 16)), -0.4, 0.0), -0.15, 0.15)
    weight_in = bell_draw(seeds[2], (HID, SPECIES), SPECIES ** -0.5, 0.375)
    weight_out = bell_draw(seeds[3], (SPECIES, HID), HID ** -0.5, 0.25)
    return dict(tracers=tracers, fluxes=fluxes, weight_in=weight_in, weight_out=weight_out)


def positive(value):
    return jnp.maximum(value, 0.0)


def negative(value):
    return jnp.minimum(value, 0.0)


def advance(padded_state, padded_x, flux_y, padded_z):
    inner = padded_state[:, 1:-1, 1:-1]
    along_x = padded_state[:, 1:-1]
    face_x = padded_x[:, 1:]
    faces_x = positive(face_x) * along_x[:, :, :-1] + negative(face_x) * along_x[:, :, 1:]
    along_z = padded_state[:, :, 1:-1]
    face_z = padded_z[1:]
    faces_z = positive(face_z) * along_z[:, :-1] + negative(face_z) * along_z[:, 1:]
    faces_y = positive(flux_y) * jnp.roll(inner, 1, 3) + negative(flux_y) * inner
    return inner + faces_x[:, :, :-1] - faces_x[:, :, 1:] + faces_y - jnp.roll(faces_y, -1, 3) + faces_z[:, :-1] - faces_z[:, 1:]


def reaction(weight_in, weight_out, level):
    flattened = level.reshape(level.shape[0], -1).astype(jnp.bfloat16)
    hidden = jax.nn.silu(jnp.dot(weight_in, flattened, preferred_element_type=jnp.float32)).astype(jnp.bfloat16)
    tendency = (0.5 * jnp.dot(weight_out, hidden, preferred_element_type=jnp.float32)).astype(jnp.bfloat16)
    return tendency.reshape(level.shape)


def reference(tracers, fluxes, weight_in, weight_out):
    shape_grid = fluxes.shape[2:]
    column = lax.broadcasted_iota(jnp.int32, shape_grid, 1)
    level_at = lax.broadcasted_iota(jnp.int32, shape_grid, 0)
    state = tracers
    for interval in range(STEPS):
        flux_x = jnp.where(column == 0, 0.0, fluxes[interval, 0])
        flux_y = fluxes[interval, 1]
        flux_z = jnp.where(level_at == 0, 0.0, fluxes[interval, 2])
        padded_x = jnp.pad(flux_x, ((0, 0), (1, 1), (0, 0)))
        padded_z = jnp.pad(flux_z, ((1, 1), (0, 0), (0, 0)))

        def single(species_row):
            padded_state = jnp.pad(species_row[None], ((0, 0), (1, 1), (1, 1), (0, 0)))
            return advance(padded_state, padded_x, flux_y, padded_z)[0]

        state = lax.map(single, state)
        tendency = lax.map(partial(reaction, weight_in, weight_out), jnp.moveaxis(state, 1, 0))
        state = state + jnp.moveaxis(tendency, 0, 1).astype(jnp.float32)
    return state
```

```python
import functools

import jax
import jax.numpy as jnp
from jax import lax
from jax.experimental import pallas as pl
from jax.experimental.pallas import tpu as pltpu
from jax.sharding import PartitionSpec as P

STEPS = 4
GROUP = 16
TILES = 16
LANES = 128
SPEC = 256
OWN = 16
BLOCK = 8
CHUNKS = 4
F32 = jnp.float32
BF16 = jnp.bfloat16
MESH = pl.DeviceIdType.MESH


def device_of(block):
    place = block // 2
    half = place // 4
    row = jnp.where(half == 0, place, 7 - place)
    return 4 * row + 2 * half + block % 2


def block_of(device):
    row = device // 4
    half = (device // 2) % 2
    place = jnp.where(half == 0, row, 7 - row)
    return 2 * place + device % 2


def transport(
    tracers, fluxes, weight_in, weight_out, back,
    turned, sent, flux_out, flux_own, flux_next, edge_out, edge_in, arrived,
    state, coeff, xs_out, xs_in, ys_out, ys_in, cells, hidden, result,
    flux_send, flux_recv, main_send, main_recv, edge_send, edge_recv,
    x_send, x_recv, y_send, y_recv, back_send, back_recv,
):
    spec = lax.axis_index("species")
    tile = lax.axis_index("tile")
    block = block_of(spec)
    right_tile = lax.rem(tile + 1, TILES)
    left_tile = lax.rem(tile + TILES - 1, TILES)
    upper = device_of(lax.rem(block + 1, GROUP))
    lower = device_of(lax.rem(block + GROUP - 1, GROUP))

    barrier = pltpu.get_barrier_semaphore()

    def greet(k, carry):
        peer = lax.rem(spec + k, GROUP)

        @pl.when(k > 0)
        def _():
            pl.semaphore_signal(barrier, inc=1, device_id=(peer, tile), device_id_type=MESH)

        pl.semaphore_signal(barrier, inc=1, device_id=(peer, left_tile), device_id_type=MESH)
        pl.semaphore_signal(barrier, inc=1, device_id=(peer, right_tile), device_id_type=MESH)
        return carry

    lax.fori_loop(0, GROUP, greet, 0)

    rows = []
    for step in range(STEPS):
        along_y = fluxes[step, 1, 0]
        rows += [fluxes[step, 0, 0], along_y, fluxes[step, 2, 0], pltpu.roll(along_y, LANES - 1, 1)]
    flux_out[...] = jnp.concatenate(rows, 0).T

    def turn(own, carry):
        turned[pl.ds(own, LANES, stride=OWN), :] = tracers[own].reshape(LANES, LANES).T
        return carry

    lax.fori_loop(0, OWN, turn, 0)

    def narrow(y, carry):
        sent[y + 1] = turned[pl.ds(y * OWN, OWN), :].astype(BF16)
        return carry

    lax.fori_loop(0, LANES, narrow, 0, unroll=8)
    sent[0] = turned[pl.ds((LANES - 1) * OWN, OWN), :].astype(BF16)
    sent[LANES + 1] = turned[pl.ds(0, OWN), :].astype(BF16)

    pl.semaphore_wait(barrier, 3 * GROUP - 1)

    def flux_copy(k, home):
        peer = lax.rem(spec + k, GROUP)
        return pltpu.make_async_remote_copy(
            src_ref=flux_out.at[pl.ds(pl.multiple_of(block_of(peer) * BLOCK, BLOCK), BLOCK)],
            dst_ref=(flux_own if home else flux_next).at[spec],
            send_sem=flux_send.at[0 if home else 1, k],
            recv_sem=flux_recv.at[0 if home else 1],
            device_id=(peer, tile if home else left_tile),
            device_id_type=MESH,
        )

    def main_copy(k):
        peer = lax.rem(spec + k, GROUP)
        return pltpu.make_async_remote_copy(
            src_ref=sent.at[pl.ds(block_of(peer) * BLOCK, BLOCK + 2)],
            dst_ref=arrived.at[:, pl.ds(pl.multiple_of(spec * OWN, OWN), OWN)],
            send_sem=main_send.at[k],
            recv_sem=main_recv,
            device_id=(peer, tile),
            device_id_type=MESH,
        )

    own_flux = pltpu.make_async_copy(
        flux_out.at[pl.ds(pl.multiple_of(block * BLOCK, BLOCK), BLOCK)], flux_own.at[spec], flux_recv.at[0]
    )
    own_main = pltpu.make_async_copy(
        sent.at[pl.ds(block * BLOCK, BLOCK + 2)],
        arrived.at[:, pl.ds(pl.multiple_of(spec * OWN, OWN), OWN)],
        main_recv,
    )

    own_flux.start()

    def send_flux(k, carry):
        @pl.when(k > 0)
        def _():
            flux_copy(k, True).start()

        flux_copy(k, False).start()
        return carry

    lax.fori_loop(0, GROUP, send_flux, 0)
    own_main.start()

    def send_main(k, carry):
        main_copy(k).start()
        return carry

    lax.fori_loop(1, GROUP, send_main, 0)

    lane = lax.broadcasted_iota(jnp.int32, (1, LANES), 1)
    at_x = lane % 8
    at_z = lane // 8

    def edge_copy(k, side):
        peer = lax.rem(spec + k, GROUP)
        return pltpu.make_async_remote_copy(
            src_ref=edge_out.at[side, block_of(peer)],
            dst_ref=edge_in.at[side, pl.ds(pl.multiple_of(spec * OWN, OWN), OWN)],
            send_sem=edge_send.at[side, k],
            recv_sem=edge_recv.at[side],
            device_id=(peer, right_tile if side == 0 else left_tile),
            device_id_type=MESH,
        )

    def pack_edges(to, carry):
        base = to * (BLOCK * OWN)
        high = jnp.zeros((OWN, LANES), F32)
        low = jnp.zeros((OWN, LANES), F32)
        for y in range(BLOCK):
            value = turned[pl.ds(base + y * OWN, OWN), :]
            high = jnp.where(at_x == y, pltpu.roll(value, (y - 7) % LANES, 1), high)
            low = jnp.where(at_x == y, pltpu.roll(value, y, 1) if y else value, low)
        edge_out[0, to] = high.astype(BF16)
        edge_out[1, to] = low.astype(BF16)
        return carry

    lax.fori_loop(0, GROUP, pack_edges, 0)

    def send_edges(k, carry):
        edge_copy(k, 0).start()
        edge_copy(k, 1).start()
        return carry

    lax.fori_loop(0, GROUP, send_edges, 0)

    pltpu.make_async_copy(flux_own, flux_own, flux_recv.at[0]).wait()
    pltpu.make_async_copy(flux_next, flux_next, flux_recv.at[1]).wait()
    for step in range(STEPS):
        fields = []
        for field in range(4):
            value = jnp.zeros((BLOCK, LANES), F32)
            for level in range(16):
                shift = (level * 8 - (step * 4 + field) * 8) % LANES
                piece = flux_own[level]
                value = jnp.where(at_z == level, pltpu.roll(piece, shift, 1) if shift else piece, value)
            fields.append(value)
        flux_x, flux_y, flux_z, flux_y_up = fields
        beyond = jnp.zeros((BLOCK, LANES), F32)
        for level in range(16):
            shift = (level * 8 + 7 - step * 32) % LANES
            beyond = jnp.where(at_z == level, pltpu.roll(flux_next[level], shift, 1), beyond)
        flux_x = jnp.where((at_x == 0) & (tile == 0), 0.0, flux_x)
        beyond = jnp.where(tile == TILES - 1, 0.0, beyond)
        flux_z = jnp.where(at_z == 0, 0.0, flux_z)
        flux_x_up = jnp.where(at_x == 7, beyond, pltpu.roll(flux_x, LANES - 1, 1))
        flux_z_up = pltpu.roll(flux_z, LANES - 8, 1)
        lows = [jnp.minimum(f, 0.0) for f in (flux_x, flux_y, flux_z)]
        highs = [jnp.maximum(f, 0.0) for f in (flux_x_up, flux_y_up, flux_z_up)]
        centre = 1.0 + (lows[0] - highs[0]) + (lows[1] - highs[1]) + (lows[2] - highs[2])
        terms = [
            centre,
            jnp.maximum(flux_x, 0.0), -jnp.minimum(flux_x_up, 0.0),
            jnp.maximum(flux_y, 0.0), -jnp.minimum(flux_y_up, 0.0),
            jnp.maximum(flux_z, 0.0), -jnp.minimum(flux_z_up, 0.0),
        ]
        for which, term in enumerate(terms):
            coeff[pl.ds(step * 64 + which, BLOCK, stride=8), :] = term

    pltpu.make_async_copy(arrived, arrived, main_recv).wait()

    def widen(row, carry):
        at = pl.ds(pl.multiple_of(row * 32, 32), 32)
        for slab in range(BLOCK + 2):
            state[0, slab, at] = arrived[slab, at].astype(F32)
        return carry

    lax.fori_loop(0, SPEC // 32, widen, 0)
    for side in range(2):
        pltpu.make_async_copy(edge_in.at[side], edge_in.at[side], edge_recv.at[side]).wait()

    def repack(row, carry):
        at = pl.multiple_of(row * 16, 16)
        for side in range(2):
            values = [edge_in[side, pl.ds(q * 64 + at, 16)].astype(F32) for q in range(4)]
            for chunk in range(CHUNKS):
                value = jnp.zeros((16, LANES), F32)
                for q in range(4):
                    shift = (2 * q - 2 * chunk) % LANES
                    moved = pltpu.roll(values[q], shift, 1) if shift else values[q]
                    value = jnp.where(at_x // 2 == q, moved, value)
                xs_in[0, chunk, side, pl.ds(at, 16)] = value.astype(BF16)
        return carry

    lax.fori_loop(0, 4, repack, 0)

    def x_copy(step, chunk, side):
        return pltpu.make_async_remote_copy(
            src_ref=xs_out.at[step, chunk, side],
            dst_ref=xs_in.at[step + 1, chunk, side],
            send_sem=x_send.at[step, chunk, side],
            recv_sem=x_recv.at[step, chunk, side],
            device_id=(spec, right_tile if side == 0 else left_tile),
            device_id_type=MESH,
        )

    def y_copy(step, side):
        return pltpu.make_async_remote_copy(
            src_ref=ys_out.at[step, side],
            dst_ref=ys_in.at[step, side],
            send_sem=y_send.at[step, side],
            recv_sem=y_recv.at[step, side],
            device_id=(upper if side == 0 else lower, tile),
            device_id_type=MESH,
        )

    def back_copy(chunk, k):
        peer = lax.rem(spec + k, GROUP)
        return pltpu.make_async_remote_copy(
            src_ref=result.at[pl.ds(2 * chunk, 2), pl.ds(pl.multiple_of(peer * OWN, OWN), OWN)],
            dst_ref=back.at[pl.ds(block * BLOCK + 2 * chunk, 2)],
            send_sem=back_send.at[chunk, k],
            recv_sem=back_recv,
            device_id=(peer, tile),
            device_id_type=MESH,
        )

    def own_back(chunk):
        return pltpu.make_async_copy(
            result.at[pl.ds(2 * chunk, 2), pl.ds(pl.multiple_of(spec * OWN, OWN), OWN)],
            back.at[pl.ds(block * BLOCK + 2 * chunk, 2)],
            back_recv,
        )

    def halo_slab(step, now, side):
        y_copy(step - 1, side).wait_recv()

        def one(row, carry):
            at = pl.ds(pl.multiple_of(row * 32, 32), 32)
            state[now, 0 if side == 0 else BLOCK + 1, at] = ys_in[step - 1, side, at].astype(F32)
            return carry

        lax.fori_loop(0, SPEC // 32, one, 0)

    def do_chunk(step, order):
        chunk = jnp.where(order == 0, 0, jnp.where(order == 1, CHUNKS - 1, order - 1))
        now = lax.rem(step, 2)
        later = 1 - now

        @pl.when(step > 0)
        def _():
            x_copy(step - 1, chunk, 0).wait_recv()
            x_copy(step - 1, chunk, 1).wait_recv()

            @pl.when(chunk == 0)
            def _():
                halo_slab(step, now, 0)

            @pl.when(chunk == CHUNKS - 1)
            def _():
                halo_slab(step, now, 1)

        for yy in range(2):
            y = 2 * chunk + yy
            table = coeff[pl.ds(pl.multiple_of((step * BLOCK + y) * 8, 8), 8), :]
            ks = [table[i:i + 1] for i in range(7)]

            def rows_of(part, carry, yy=yy, y=y, ks=ks):
                off = pl.multiple_of(part * 32, 32)
                halo_l = xs_in[step, chunk, 0, pl.ds(off, 32)].astype(F32)
                halo_r = xs_in[step, chunk, 1, pl.ds(off, 32)].astype(F32)
                for q in range(4):
                    slot = 2 * q + yy
                    at = pl.ds(off + q * 64, 32)
                    here = state[now, y + 1, at]
                    from_l = pltpu.roll(halo_l, LANES - slot, 1) if slot else halo_l
                    from_r = pltpu.roll(halo_r, 7 - slot, 1) if slot < 7 else halo_r
                    left = jnp.where(at_x == 0, from_l, pltpu.roll(here, 1, 1))
                    right = jnp.where(at_x == 7, from_r, pltpu.roll(here, LANES - 1, 1))
                    new = ks[0] * here + ks[1] * left + ks[2] * right
                    new += ks[3] * state[now, y, at] + ks[4] * state[now, y + 2, at]
                    new += ks[5] * pltpu.roll(here, 8, 1) + ks[6] * pltpu.roll(here, LANES - 8, 1)
                    state[later, y + 1, at] = new
                    cells[at, yy * LANES:(yy + 1) * LANES] = new.astype(BF16)
                return carry

            lax.fori_loop(0, 2, rows_of, 0)

        pre = jnp.dot(weight_in[...], cells[...], preferred_element_type=F32)
        hidden[...] = (0.5 * pre * (1.0 + jnp.tanh(0.5 * pre))).astype(BF16)
        change = (0.5 * jnp.dot(weight_out[...], hidden[...], preferred_element_type=F32)).astype(BF16).astype(F32)
        for yy in range(2):
            state[later, 2 * chunk + yy + 1] += change[:, yy * LANES:(yy + 1) * LANES]

        @pl.when(step < STEPS - 1)
        def _():
            def pack(part, carry):
                off = pl.multiple_of(part * 16, 16)
                high = jnp.zeros((16, LANES), F32)
                low = jnp.zeros((16, LANES), F32)
                for q in range(4):
                    for yy in range(2):
                        slot = 2 * q + yy
                        value = state[later, 2 * chunk + yy + 1, pl.ds(off + q * 64, 16)]
                        high = jnp.where(at_x == slot, pltpu.roll(value, (slot - 7) % LANES, 1), high)
                        low = jnp.where(at_x == slot, pltpu.roll(value, slot, 1) if slot else value, low)
                xs_out[step, chunk, 0, pl.ds(off, 16)] = high.astype(BF16)
                xs_out[step, chunk, 1, pl.ds(off, 16)] = low.astype(BF16)
                return carry

            lax.fori_loop(0, 4, pack, 0)
            x_copy(step, chunk, 0).start()
            x_copy(step, chunk, 1).start()

            @pl.when(chunk == 0)
            def _():
                ys_out[step, 1] = state[later, 1].astype(BF16)
                y_copy(step, 1).start()

            @pl.when(chunk == CHUNKS - 1)
            def _():
                ys_out[step, 0] = state[later, BLOCK].astype(BF16)
                y_copy(step, 0).start()

        @pl.when(step == STEPS - 1)
        def _():
            for yy in range(2):
                result[2 * chunk + yy] = state[later, 2 * chunk + yy + 1].astype(BF16)
            own_back(chunk).start()

            def send_back(k, carry):
                back_copy(chunk, k).start()
                return carry

            lax.fori_loop(1, GROUP, send_back, 0)

    def do_step(step, carry):
        def one(order, inner):
            do_chunk(step, order)
            return inner

        lax.fori_loop(0, CHUNKS, one, 0)
        return carry

    lax.fori_loop(0, STEPS, do_step, 0)

    def sent_out(k, carry):
        flux_copy(k, False).wait_send()
        edge_copy(k, 0).wait_send()
        edge_copy(k, 1).wait_send()

        @pl.when(k > 0)
        def _():
            flux_copy(k, True).wait_send()
            main_copy(k).wait_send()

        return carry

    lax.fori_loop(0, GROUP, sent_out, 0)
    for step in range(STEPS - 1):
        for side in range(2):
            y_copy(step, side).wait_send()
            for chunk in range(CHUNKS):
                x_copy(step, chunk, side).wait_send()

    def back_out(k, carry):
        for chunk in range(CHUNKS):
            back_copy(chunk, k).wait_send()
        return carry

    lax.fori_loop(1, GROUP, back_out, 0)
    pltpu.make_async_copy(back, back, back_recv).wait()


def turn_back(back, out, wide):
    def widen(y, carry):
        wide[pl.ds(pl.multiple_of(y * OWN, OWN), OWN), :] = back[y].astype(F32)
        return carry

    lax.fori_loop(0, LANES, widen, 0, unroll=8)

    def one(own, carry):
        out[own] = wide[pl.ds(own, LANES, stride=OWN), :].T.reshape(16, 8, LANES)
        return carry

    lax.fori_loop(0, OWN, one, 0)


def per_device(tracers, fluxes, weight_in, weight_out):
    vmem = pl.BlockSpec(memory_space=pltpu.VMEM)
    dma = pltpu.SemaphoreType.DMA
    back = pl.pallas_call(
        transport,
        out_shape=jax.ShapeDtypeStruct((LANES, OWN, LANES), BF16),
        in_specs=[vmem] * 4,
        out_specs=pl.BlockSpec(memory_space=pl.ANY),
        scratch_shapes=[
            pltpu.VMEM((LANES * OWN, LANES), F32),
            pltpu.VMEM((LANES + 2, OWN, LANES), BF16),
            pltpu.VMEM((LANES, LANES), F32),
            pltpu.VMEM((GROUP, BLOCK, LANES), F32),
            pltpu.VMEM((GROUP, BLOCK, LANES), F32),
            pltpu.VMEM((2, GROUP, OWN, LANES), BF16),
            pltpu.VMEM((2, SPEC, LANES), BF16),
            pltpu.VMEM((BLOCK + 2, SPEC, LANES), BF16),
            pltpu.VMEM((2, BLOCK + 2, SPEC, LANES), F32),
            pltpu.VMEM((STEPS * 64, LANES), F32),
            pltpu.VMEM((STEPS - 1, CHUNKS, 2, 64, LANES), BF16),
            pltpu.VMEM((STEPS, CHUNKS, 2, 64, LANES), BF16),
            pltpu.VMEM((STEPS - 1, 2, SPEC, LANES), BF16),
            pltpu.VMEM((STEPS - 1, 2, SPEC, LANES), BF16),
            pltpu.VMEM((SPEC, 2 * LANES), BF16),
            pltpu.VMEM((2 * SPEC, 2 * LANES), BF16),
            pltpu.VMEM((BLOCK, SPEC, LANES), BF16),
            dma((2, GROUP)), dma((2,)), dma((GROUP,)), dma(()), dma((2, GROUP)), dma((2,)),
            dma((STEPS - 1, CHUNKS, 2)), dma((STEPS - 1, CHUNKS, 2)), dma((STEPS - 1, 2)), dma((STEPS - 1, 2)),
            dma((CHUNKS, GROUP)), dma(()),
        ],
        compiler_params=pltpu.CompilerParams(collective_id=0, has_side_effects=True, vmem_limit_bytes=48 * 2**20),
        name="transport",
    )(tracers, fluxes, weight_in, weight_out)
    return pl.pallas_call(
        turn_back,
        out_shape=jax.ShapeDtypeStruct((OWN, 16, 8, LANES), F32),
        in_specs=[vmem],
        out_specs=vmem,
        scratch_shapes=[pltpu.VMEM((LANES * OWN, LANES), F32)],
        name="turn_back",
    )(back)


def solution(mesh):
    placed = (P("species", None, "tile", None), P(None, None, "species", "tile", None), P(), P())
    return jax.shard_map(
        per_device,
        mesh=mesh,
        in_specs=placed,
        out_specs=P("species", None, "tile", None),
        check_vma=False,
    )
```

```python
import jax
import jax.numpy as jnp
from jax import lax
from jax.experimental import pallas as pl
from jax.experimental.pallas import tpu as pltpu
from jax.sharding import PartitionSpec as P

STEPS = 4
GROUP = 16
TILES = 16
LANES = 128
PAIR = 2 * LANES
SPEC = 256
HID = 512
OWN = 16
BLOCK = 8
CHUNKS = 4
ORDER = (0, 3, 1, 2)
F32 = jnp.float32
BF16 = jnp.bfloat16
MESH = pl.DeviceIdType.MESH


def device_of(block):
    place = block // 2
    half = place // 4
    row = jnp.where(half == 0, place, 7 - place)
    return 4 * row + 2 * half + block % 2


def block_of(device):
    row = device // 4
    half = (device // 2) % 2
    place = jnp.where(half == 0, row, 7 - row)
    return 2 * place + device % 2


def transport(
    tracers_hbm, fluxes_hbm, weight_in_hbm, weight_out_hbm, out,
    tracers, fluxes, weight_in, weight_out, turned, sent, flux_out, flux_in, beyond_out, beyond_in,
    narrow, master, coeff, band, xs_out, xs_in, ys_in, hidden, back,
    load, flux_send, flux_recv, beyond_sem, main_send, main_recv,
    x_send, x_recv, y_send, y_recv, back_send, back_recv,
):
    spec = lax.axis_index("species")
    tile = lax.axis_index("tile")
    block = block_of(spec)
    right_tile = lax.rem(tile + 1, TILES)
    left_tile = lax.rem(tile + TILES - 1, TILES)
    upper = device_of(lax.rem(block + 1, GROUP))
    lower = device_of(lax.rem(block + GROUP - 1, GROUP))
    mine = pl.ds(pl.multiple_of(spec * OWN, OWN), OWN)

    loads = [
        pltpu.make_async_copy(fluxes_hbm, fluxes, load.at[0]),
        pltpu.make_async_copy(tracers_hbm, tracers, load.at[1]),
        pltpu.make_async_copy(weight_in_hbm, weight_in, load.at[2]),
        pltpu.make_async_copy(weight_out_hbm, weight_out, load.at[3]),
    ]
    for copy in loads:
        copy.start()

    barrier = pltpu.get_barrier_semaphore()

    def greet(k, carry):
        pl.semaphore_signal(
            barrier, inc=1, device_id=(lax.rem(spec + k, GROUP), tile), device_id_type=MESH
        )
        return carry

    lax.fori_loop(1, GROUP, greet, 0)
    for side_tile in (left_tile, right_tile):
        pl.semaphore_signal(barrier, inc=1, device_id=(spec, side_tile), device_id_type=MESH)

    loads[0].wait()
    rows = []
    for step in range(STEPS):
        along_y = fluxes[step, 1, 0]
        rows += [fluxes[step, 0, 0], along_y, fluxes[step, 2, 0], pltpu.roll(along_y, LANES - 1, 1)]
    flux_turned = jnp.concatenate(rows, 0).T
    for to in range(GROUP):
        flux_out[to] = flux_turned[to * BLOCK:(to + 1) * BLOCK].astype(BF16)

    loads[1].wait()

    def turn(part, carry):
        for i in range(4):
            own = part * 4 + i
            turned[pl.ds(own, LANES, stride=OWN), :] = tracers[own].reshape(LANES, LANES).T
        return carry

    lax.fori_loop(0, OWN // 4, turn, 0)

    def narrowed(y, carry):
        for yy in range(2):
            sent[y, :, yy * LANES:(yy + 1) * LANES] = turned[
                pl.ds(pl.multiple_of((2 * y + yy) * OWN, OWN), OWN), :
            ].astype(BF16)
        return carry

    lax.fori_loop(0, LANES // 2, narrowed, 0, unroll=8)

    pl.semaphore_wait(barrier, GROUP + 1)

    def flux_copy(k):
        peer = lax.rem(spec + k, GROUP)
        return pltpu.make_async_remote_copy(
            src_ref=flux_out.at[block_of(peer)],
            dst_ref=flux_in.at[spec],
            send_sem=flux_send.at[k],
            recv_sem=flux_recv,
            device_id=(peer, tile),
            device_id_type=MESH,
        )

    def main_copy(chunk, k):
        peer = lax.rem(spec + k, GROUP)
        return pltpu.make_async_remote_copy(
            src_ref=sent.at[block_of(peer) * CHUNKS + chunk],
            dst_ref=narrow.at[0, chunk, mine],
            send_sem=main_send.at[chunk, k],
            recv_sem=main_recv.at[chunk],
            device_id=(peer, tile),
            device_id_type=MESH,
        )

    pltpu.make_async_copy(flux_out.at[block], flux_in.at[spec], flux_recv).start()

    def send_flux(k, carry):
        flux_copy(k).start()
        return carry

    lax.fori_loop(1, GROUP, send_flux, 0)
    for chunk in ORDER:
        pltpu.make_async_copy(
            sent.at[block * CHUNKS + chunk], narrow.at[0, chunk, mine], main_recv.at[chunk]
        ).start()

        def send_main(k, carry, chunk=chunk):
            main_copy(chunk, k).start()
            return carry

        lax.fori_loop(1, GROUP, send_main, 0)

    loads[2].wait()
    loads[3].wait()
    weight_in[...] = weight_in[...] * jnp.asarray(0.5, BF16)
    weight_out[...] = weight_out[...] * jnp.asarray(0.5, BF16)

    lane = lax.broadcasted_iota(jnp.int32, (1, LANES), 1)
    at_x = lane % 8
    at_z = lane // 8

    pltpu.make_async_copy(flux_in, flux_in, flux_recv).wait()
    beyond_copy = pltpu.make_async_remote_copy(
        src_ref=beyond_out,
        dst_ref=beyond_in,
        send_sem=beyond_sem.at[0],
        recv_sem=beyond_sem.at[1],
        device_id=(spec, left_tile),
        device_id_type=MESH,
    )
    pieces = [flux_in[level].astype(F32) for level in range(16)]

    def field_of(step, field):
        value = jnp.zeros((BLOCK, LANES), F32)
        for level in range(16):
            shift = (level * 8 - (step * 4 + field) * 8) % LANES
            value = jnp.where(at_z == level, pltpu.roll(pieces[level], shift, 1) if shift else pieces[level], value)
        return value

    for step in range(STEPS):
        beyond_out[step] = jnp.where((at_x == 0) & (tile == 0), 0.0, field_of(step, 0))
    beyond_copy.start()
    others = [[field_of(step, field) for field in (1, 2, 3)] for step in range(STEPS)]
    beyond_copy.wait_recv()
    for step in range(STEPS):
        flux_x = beyond_out[step]
        flux_y, flux_z, flux_y_up = others[step]
        beyond = jnp.where(tile == TILES - 1, 0.0, pltpu.roll(beyond_in[step], 7, 1))
        flux_z = jnp.where(at_z == 0, 0.0, flux_z)
        flux_x_up = jnp.where(at_x == 7, beyond, pltpu.roll(flux_x, LANES - 1, 1))
        flux_z_up = pltpu.roll(flux_z, LANES - 8, 1)
        lows = [jnp.minimum(f, 0.0) for f in (flux_x, flux_y, flux_z)]
        highs = [jnp.maximum(f, 0.0) for f in (flux_x_up, flux_y_up, flux_z_up)]
        west, east = jnp.maximum(flux_x, 0.0), -jnp.minimum(flux_x_up, 0.0)
        terms = [
            (lows[0] - highs[0]) + (lows[1] - highs[1]) + (lows[2] - highs[2]),
            jnp.where(at_x == 0, 0.0, west),
            jnp.where(at_x == 7, 0.0, east),
            jnp.maximum(flux_z, 0.0),
            -jnp.minimum(flux_z_up, 0.0),
            jnp.maximum(flux_y, 0.0),
            -jnp.minimum(flux_y_up, 0.0),
            jnp.where(at_x == 0, west, jnp.where(at_x == 7, east, 0.0)),
        ]
        for which, term in enumerate(terms):
            coeff[pl.ds(step * 64 + which, BLOCK, stride=8), :] = term

    def bands(part, carry):
        at = pl.multiple_of((part % 8) * 16, 16)
        step = part // 8
        away = lax.broadcasted_iota(jnp.int32, (16, LANES), 1) - (
            lax.broadcasted_iota(jnp.int32, (16, LANES), 0) + at
        )
        masks = [away == d for d in (0, 1, -1, 8, -8)]
        for chunk in range(CHUNKS):
            for yy in range(2):
                table = coeff[pl.ds(pl.multiple_of((step * BLOCK + 2 * chunk + yy) * 8, 8), 8), :]
                value = jnp.zeros((16, LANES), F32)
                for i in range(5):
                    value = jnp.where(masks[i], table[i:i + 1], value)
                cross = jnp.where(masks[0], table[6:7] if yy == 0 else table[5:6], 0.0)
                lanes = slice(yy * LANES, (yy + 1) * LANES)
                band[step, chunk, pl.ds(yy * LANES + at, 16), lanes] = value.astype(BF16)
                band[step, chunk, pl.ds((1 - yy) * LANES + at, 16), lanes] = cross.astype(BF16)
        return carry

    lax.fori_loop(0, 8 * STEPS, bands, 0)

    def x_copy(step, chunk, side):
        return pltpu.make_async_remote_copy(
            src_ref=xs_out.at[step, chunk, side],
            dst_ref=xs_in.at[step, chunk, side],
            send_sem=x_send.at[step, chunk, side],
            recv_sem=x_recv.at[step, chunk, side],
            device_id=(spec, right_tile if side == 0 else left_tile),
            device_id_type=MESH,
        )

    def y_copy(step, side):
        return pltpu.make_async_remote_copy(
            src_ref=narrow.at[step, CHUNKS - 1 if side == 0 else 0, :, pl.ds(LANES if side == 0 else 0, LANES)],
            dst_ref=ys_in.at[step, side],
            send_sem=y_send.at[step, side],
            recv_sem=y_recv.at[step, side],
            device_id=(upper if side == 0 else lower, tile),
            device_id_type=MESH,
        )

    def publish(step, chunk):
        if chunk == 0:
            y_copy(step, 1).start()
        if chunk == CHUNKS - 1:
            y_copy(step, 0).start()
        for off in range(0, 64, 16):
            high = jnp.zeros((16, LANES), F32)
            low = jnp.zeros((16, LANES), F32)
            for q in range(4):
                for yy in range(2):
                    slot = 2 * q + yy
                    value = master[chunk, q * 64 + off:q * 64 + off + 16, yy * LANES:(yy + 1) * LANES]
                    high = jnp.where(at_x == slot, pltpu.roll(value, (slot - 7) % LANES, 1) if slot < 7 else value, high)
                    low = jnp.where(at_x == slot, pltpu.roll(value, slot, 1) if slot else value, low)
            xs_out[step, chunk, 0, off:off + 16] = high.astype(BF16)
            xs_out[step, chunk, 1, off:off + 16] = low.astype(BF16)
        x_copy(step, chunk, 0).start()
        x_copy(step, chunk, 1).start()

    for chunk in ORDER:
        pltpu.make_async_copy(narrow.at[0, chunk], narrow.at[0, chunk], main_recv.at[chunk]).wait()
        master[chunk] = narrow[0, chunk].astype(F32)
        publish(0, chunk)

    def back_copy(chunk, k):
        peer = lax.rem(spec + k, GROUP)
        return pltpu.make_async_remote_copy(
            src_ref=narrow.at[STEPS, chunk, pl.ds(pl.multiple_of(peer * OWN, OWN), OWN)],
            dst_ref=back.at[chunk, block],
            send_sem=back_send.at[chunk, k],
            recv_sem=back_recv.at[chunk],
            device_id=(peer, tile),
            device_id_type=MESH,
        )

    def do_chunk(step, chunk):
        x_copy(step, chunk, 0).wait_recv()
        x_copy(step, chunk, 1).wait_recv()
        if chunk == 0:
            y_copy(step, 0).wait_recv()
        if chunk == CHUNKS - 1:
            y_copy(step, 1).wait_recv()

        inner = jnp.dot(narrow[step, chunk], band[step, chunk], preferred_element_type=F32)
        tables = [
            coeff[pl.ds(pl.multiple_of((step * BLOCK + 2 * chunk + yy) * 8, 8), 8), :] for yy in range(2)
        ]
        for off in range(0, 64, 32):
            halo_l = xs_in[step, chunk, 0, off:off + 32].astype(F32)
            halo_r = xs_in[step, chunk, 1, off:off + 32].astype(F32)
            for q in range(4):
                for yy in range(2):
                    slot = 2 * q + yy
                    at = slice(off + q * 64, off + q * 64 + 32)
                    lanes = slice(yy * LANES, (yy + 1) * LANES)
                    if yy == 0:
                        outer = ys_in[step, 0, at] if chunk == 0 else narrow[step, chunk - 1, at, LANES:]
                        k_outer = tables[0][5:6]
                    else:
                        outer = ys_in[step, 1, at] if chunk == CHUNKS - 1 else narrow[step, chunk + 1, at, :LANES]
                        k_outer = tables[1][6:7]
                    from_l = pltpu.roll(halo_l, LANES - slot, 1) if slot else halo_l
                    from_r = pltpu.roll(halo_r, 7 - slot, 1) if slot < 7 else halo_r
                    new = master[chunk, at, lanes] + inner[at, lanes] + k_outer * outer.astype(F32)
                    new += tables[yy][7:8] * jnp.where(at_x == 0, from_l, from_r)
                    master[chunk, at, lanes] = new
                    narrow[step + 1, chunk, at, lanes] = new.astype(BF16)

        cells = narrow[step + 1, chunk]
        for part in range(4):
            rows_at = slice(part * LANES, (part + 1) * LANES)
            pre = jnp.dot(weight_in[rows_at], cells, preferred_element_type=F32)
            hidden[rows_at] = (pre + pre * jnp.tanh(pre)).astype(BF16)
        after = master[chunk] + jnp.dot(weight_out[...], hidden[...], preferred_element_type=F32)
        master[chunk] = after
        narrow[step + 1, chunk] = after.astype(BF16)

        @pl.when(step < STEPS - 1)
        def _():
            publish(step + 1, chunk)

        @pl.when(step == STEPS - 1)
        def _():
            pltpu.make_async_copy(narrow.at[STEPS, chunk, mine], back.at[chunk, block], back_recv.at[chunk]).start()

            def send_back(k, carry):
                back_copy(chunk, k).start()
                return carry

            lax.fori_loop(1, GROUP, send_back, 0)

    def do_step(step, carry):
        for chunk in ORDER:
            do_chunk(step, chunk)
        return carry

    lax.fori_loop(0, STEPS, do_step, 0)

    def sent_out(k, carry):
        flux_copy(k).wait_send()
        for chunk in range(CHUNKS):
            main_copy(chunk, k).wait_send()
        return carry

    lax.fori_loop(1, GROUP, sent_out, 0)
    beyond_copy.wait_send()

    def halos_out(step, carry):
        for side in range(2):
            y_copy(step, side).wait_send()
            for chunk in range(CHUNKS):
                x_copy(step, chunk, side).wait_send()
        return carry

    lax.fori_loop(0, STEPS, halos_out, 0)

    for chunk in ORDER:
        pltpu.make_async_copy(back.at[chunk], back.at[chunk], back_recv.at[chunk]).wait()

        def widen(of, carry, chunk=chunk):
            for yy in range(2):
                y = of * BLOCK + 2 * chunk + yy
                turned[pl.ds(pl.multiple_of(y * OWN, OWN), OWN), :] = back[
                    chunk, of, :, yy * LANES:(yy + 1) * LANES
                ].astype(F32)
            return carry

        lax.fori_loop(0, GROUP, widen, 0, unroll=4)

    def turn_back(part, carry):
        for i in range(4):
            own = part * 4 + i
            out[own] = turned[pl.ds(own, LANES, stride=OWN), :].T.reshape(16, 8, LANES)
        return carry

    lax.fori_loop(0, OWN // 4, turn_back, 0)

    def back_out(k, carry):
        for chunk in range(CHUNKS):
            back_copy(chunk, k).wait_send()
        return carry

    lax.fori_loop(1, GROUP, back_out, 0)


def per_device(tracers, fluxes, weight_in, weight_out):
    dma = pltpu.SemaphoreType.DMA
    return pl.pallas_call(
        transport,
        out_shape=jax.ShapeDtypeStruct(tracers.shape, F32),
        in_specs=[pl.BlockSpec(memory_space=pltpu.HBM)] * 4,
        out_specs=pl.BlockSpec(memory_space=pltpu.VMEM),
        scratch_shapes=[
            pltpu.VMEM(tracers.shape, F32),
            pltpu.VMEM(fluxes.shape, F32),
            pltpu.VMEM((HID, SPEC), BF16),
            pltpu.VMEM((SPEC, HID), BF16),
            pltpu.VMEM((LANES * OWN, LANES), F32),
            pltpu.VMEM((LANES // 2, OWN, PAIR), BF16),
            pltpu.VMEM((GROUP, BLOCK, LANES), BF16),
            pltpu.VMEM((GROUP, BLOCK, LANES), BF16),
            pltpu.VMEM((STEPS, BLOCK, LANES), F32),
            pltpu.VMEM((STEPS, BLOCK, LANES), F32),
            pltpu.VMEM((STEPS + 1, CHUNKS, SPEC, PAIR), BF16),
            pltpu.VMEM((CHUNKS, SPEC, PAIR), F32),
            pltpu.VMEM((STEPS * 64, LANES), F32),
            pltpu.VMEM((STEPS, CHUNKS, PAIR, PAIR), BF16),
            pltpu.VMEM((STEPS, CHUNKS, 2, 64, LANES), BF16),
            pltpu.VMEM((STEPS, CHUNKS, 2, 64, LANES), BF16),
            pltpu.VMEM((STEPS, 2, SPEC, LANES), BF16),
            pltpu.VMEM((HID, PAIR), BF16),
            pltpu.VMEM((CHUNKS, GROUP, OWN, PAIR), BF16),
            dma((4,)), dma((GROUP,)), dma(()), dma((2,)), dma((CHUNKS, GROUP)), dma((CHUNKS,)),
            dma((STEPS, CHUNKS, 2)), dma((STEPS, CHUNKS, 2)), dma((STEPS, 2)), dma((STEPS, 2)),
            dma((CHUNKS, GROUP)), dma((CHUNKS,)),
        ],
        compiler_params=pltpu.CompilerParams(collective_id=0, has_side_effects=True, vmem_limit_bytes=67043328),
        name="transport",
    )(tracers, fluxes, weight_in, weight_out)


def solution(mesh):
    placed = (P("species", None, "tile", None), P(None, None, "species", "tile", None), P(), P())
    return jax.shard_map(
        per_device,
        mesh=mesh,
        in_specs=placed,
        out_specs=P("species", None, "tile", None),
        check_vma=False,
    )
```

```python
import jax
import jax.numpy as jnp
from jax import lax
from jax.experimental import pallas as pl
from jax.experimental.pallas import tpu as pltpu
from jax.sharding import PartitionSpec as P

STEPS = 4
GROUP = 16
TILES = 16
LANES = 128
PAIR = 2 * LANES
SPEC = 256
HID = 512
OWN = 16
BLOCK = 8
CHUNKS = 4
ORDER = (0, 3, 1, 2)
PEERS = (8, 4, 12, 2, 9, 5, 13, 3, 10, 6, 14, 1, 11, 7, 15)
F32 = jnp.float32
BF16 = jnp.bfloat16
MESH = pl.DeviceIdType.MESH


def device_of(block):
    place = block // 2
    half = place // 4
    row = jnp.where(half == 0, place, 7 - place)
    return 4 * row + 2 * half + block % 2


def block_of(device):
    row = device // 4
    half = (device // 2) % 2
    place = jnp.where(half == 0, row, 7 - row)
    return 2 * place + device % 2


def transport(
    tracers_hbm, fluxes_hbm, weight_in_hbm, weight_out_hbm, back,
    tracers, fluxes, weight_in, weight_out, turned, sent, flux_out, flux_in, beyond_out, beyond_in,
    narrow, master, coeff, band, xs_out, xs_in, ys_in, hidden,
    load, flux_send, flux_recv, beyond_sem, main_send, main_recv,
    x_send, x_recv, y_send, y_recv, back_send, back_recv,
):
    spec = lax.axis_index("species")
    tile = lax.axis_index("tile")
    block = block_of(spec)
    right_tile = lax.rem(tile + 1, TILES)
    left_tile = lax.rem(tile + TILES - 1, TILES)
    upper = device_of(lax.rem(block + 1, GROUP))
    lower = device_of(lax.rem(block + GROUP - 1, GROUP))
    mine = pl.ds(pl.multiple_of(spec * OWN, OWN), OWN)

    loads = [
        pltpu.make_async_copy(fluxes_hbm, fluxes, load.at[0]),
        pltpu.make_async_copy(weight_in_hbm, weight_in, load.at[1]),
        pltpu.make_async_copy(weight_out_hbm, weight_out, load.at[2]),
    ]
    quarters = [
        pltpu.make_async_copy(tracers_hbm.at[pl.ds(4 * i, 4)], tracers.at[pl.ds(4 * i, 4)], load.at[3 + i])
        for i in range(4)
    ]
    loads = loads[:1] + quarters + loads[1:]
    for copy in loads:
        copy.start()

    barrier = pltpu.get_barrier_semaphore()

    def greet(k, carry):
        pl.semaphore_signal(
            barrier, inc=1, device_id=(lax.rem(spec + k, GROUP), tile), device_id_type=MESH
        )
        return carry

    lax.fori_loop(1, GROUP, greet, 0)
    has_side = (tile > 0, tile < TILES - 1)
    side_tiles = (left_tile, right_tile)
    for side in range(2):

        @pl.when(has_side[side])
        def _(side=side):
            pl.semaphore_signal(barrier, inc=1, device_id=(spec, side_tiles[side]), device_id_type=MESH)

        @pl.when(jnp.logical_not(has_side[side]))
        def _(side=side):
            xs_in[:, :, side] = jnp.zeros((STEPS, CHUNKS, 64, LANES), BF16)
            if side == 1:
                beyond_in[...] = jnp.zeros((STEPS, BLOCK, LANES), F32)

    loads[0].wait()
    rows = []
    for step in range(STEPS):
        along_y = fluxes[step, 1, 0]
        rows += [fluxes[step, 0, 0], along_y, fluxes[step, 2, 0], pltpu.roll(along_y, LANES - 1, 1)]
    flux_turned = jnp.concatenate(rows, 0).T
    for to in range(GROUP):
        flux_out[to] = flux_turned[to * BLOCK:(to + 1) * BLOCK].astype(BF16)

    for part in range(4):
        quarters[part].wait()
        for i in range(4):
            own = part * 4 + i
            turned[pl.ds(own, LANES, stride=OWN), :] = tracers[own].reshape(LANES, LANES).T

    def narrowed(y, carry):
        for yy in range(2):
            sent[y, :, yy * LANES:(yy + 1) * LANES] = turned[
                pl.ds(pl.multiple_of((2 * y + yy) * OWN, OWN), OWN), :
            ].astype(BF16)
        return carry

    lax.fori_loop(0, LANES // 2, narrowed, 0, unroll=8)

    pl.semaphore_wait(barrier, GROUP - 1 + has_side[0].astype(jnp.int32) + has_side[1].astype(jnp.int32))

    def flux_copy(k):
        peer = lax.rem(spec + k, GROUP)
        return pltpu.make_async_remote_copy(
            src_ref=flux_out.at[block_of(peer)],
            dst_ref=flux_in.at[spec],
            send_sem=flux_send,
            recv_sem=flux_recv,
            device_id=(peer, tile),
            device_id_type=MESH,
        )

    def main_copy(chunk, k):
        peer = lax.rem(spec + k, GROUP)
        return pltpu.make_async_remote_copy(
            src_ref=sent.at[block_of(peer) * CHUNKS + chunk],
            dst_ref=narrow.at[0, chunk, mine],
            send_sem=main_send,
            recv_sem=main_recv.at[chunk],
            device_id=(peer, tile),
            device_id_type=MESH,
        )

    pltpu.make_async_copy(flux_out.at[block], flux_in.at[spec], flux_recv).start()

    for k in PEERS:
        flux_copy(k).start()
    for chunk in ORDER:
        pltpu.make_async_copy(
            sent.at[block * CHUNKS + chunk], narrow.at[0, chunk, mine], main_recv.at[chunk]
        ).start()
        for k in PEERS:
            main_copy(chunk, k).start()

    loads[5].wait()
    loads[6].wait()
    weight_in[...] = weight_in[...] * jnp.asarray(0.5, BF16)
    weight_out[...] = weight_out[...] * jnp.asarray(0.5, BF16)

    lane = lax.broadcasted_iota(jnp.int32, (1, LANES), 1)
    at_x = lane % 8
    at_z = lane // 8

    pltpu.make_async_copy(flux_in, flux_in, flux_recv).wait()
    beyond_copy = pltpu.make_async_remote_copy(
        src_ref=beyond_out,
        dst_ref=beyond_in,
        send_sem=beyond_sem.at[0],
        recv_sem=beyond_sem.at[1],
        device_id=(spec, left_tile),
        device_id_type=MESH,
    )
    pieces = [flux_in[level].astype(F32) for level in range(16)]

    def field_of(step, field):
        value = jnp.zeros((BLOCK, LANES), F32)
        for level in range(16):
            shift = (level * 8 - (step * 4 + field) * 8) % LANES
            value = jnp.where(at_z == level, pltpu.roll(pieces[level], shift, 1) if shift else pieces[level], value)
        return value

    for step in range(STEPS):
        beyond_out[step] = jnp.where((at_x == 0) & (tile == 0), 0.0, field_of(step, 0))

    @pl.when(has_side[0])
    def _():
        beyond_copy.start()

    others = [[field_of(step, field) for field in (1, 2, 3)] for step in range(STEPS)]

    @pl.when(has_side[1])
    def _():
        beyond_copy.wait_recv()

    for step in range(STEPS):
        flux_x = beyond_out[step]
        flux_y, flux_z, flux_y_up = others[step]
        beyond = jnp.where(tile == TILES - 1, 0.0, pltpu.roll(beyond_in[step], 7, 1))
        flux_z = jnp.where(at_z == 0, 0.0, flux_z)
        flux_x_up = jnp.where(at_x == 7, beyond, pltpu.roll(flux_x, LANES - 1, 1))
        flux_z_up = pltpu.roll(flux_z, LANES - 8, 1)
        lows = [jnp.minimum(f, 0.0) for f in (flux_x, flux_y, flux_z)]
        highs = [jnp.maximum(f, 0.0) for f in (flux_x_up, flux_y_up, flux_z_up)]
        west, east = jnp.maximum(flux_x, 0.0), -jnp.minimum(flux_x_up, 0.0)
        terms = [
            (lows[0] - highs[0]) + (lows[1] - highs[1]) + (lows[2] - highs[2]),
            jnp.where(at_x == 0, 0.0, west),
            jnp.where(at_x == 7, 0.0, east),
            jnp.maximum(flux_z, 0.0),
            -jnp.minimum(flux_z_up, 0.0),
            jnp.maximum(flux_y, 0.0),
            -jnp.minimum(flux_y_up, 0.0),
            jnp.where(at_x == 0, west, jnp.where(at_x == 7, east, 0.0)),
        ]
        for which, term in enumerate(terms):
            coeff[pl.ds(step * 64 + which, BLOCK, stride=8), :] = term

    def bands(part, carry):
        at = pl.multiple_of((part % 8) * 16, 16)
        step = part // 8
        away = lax.broadcasted_iota(jnp.int32, (16, LANES), 1) - (
            lax.broadcasted_iota(jnp.int32, (16, LANES), 0) + at
        )
        masks = [away == d for d in (0, 1, -1, 8, -8)]
        for chunk in range(CHUNKS):
            for yy in range(2):
                table = coeff[pl.ds(pl.multiple_of((step * BLOCK + 2 * chunk + yy) * 8, 8), 8), :]
                value = jnp.zeros((16, LANES), F32)
                for i in range(5):
                    value = jnp.where(masks[i], table[i:i + 1], value)
                cross = jnp.where(masks[0], table[6:7] if yy == 0 else table[5:6], 0.0)
                lanes = slice(yy * LANES, (yy + 1) * LANES)
                band[step, chunk, pl.ds(yy * LANES + at, 16), lanes] = value.astype(BF16)
                band[step, chunk, pl.ds((1 - yy) * LANES + at, 16), lanes] = cross.astype(BF16)
        return carry

    lax.fori_loop(0, 8 * STEPS, bands, 0)

    def x_copy(step, chunk, side):
        return pltpu.make_async_remote_copy(
            src_ref=xs_out.at[side, step, chunk],
            dst_ref=xs_in.at[step, chunk, side],
            send_sem=x_send.at[side],
            recv_sem=x_recv.at[step, chunk],
            device_id=(spec, right_tile if side == 0 else left_tile),
            device_id_type=MESH,
        )

    def y_copy(step, side):
        return pltpu.make_async_remote_copy(
            src_ref=narrow.at[step, CHUNKS - 1 if side == 0 else 0, :, pl.ds(LANES if side == 0 else 0, LANES)],
            dst_ref=ys_in.at[step, side],
            send_sem=y_send,
            recv_sem=y_recv.at[step, side],
            device_id=(upper if side == 0 else lower, tile),
            device_id_type=MESH,
        )

    def publish(step, chunk):
        if chunk == 0:
            y_copy(step, 1).start()
        if chunk == CHUNKS - 1:
            y_copy(step, 0).start()
        for off in range(0, 64, 16):
            high = jnp.zeros((16, LANES), F32)
            low = jnp.zeros((16, LANES), F32)
            for q in range(4):
                for yy in range(2):
                    slot = 2 * q + yy
                    value = master[chunk, q * 64 + off:q * 64 + off + 16, yy * LANES:(yy + 1) * LANES]
                    high = jnp.where(at_x == slot, pltpu.roll(value, (slot - 7) % LANES, 1) if slot < 7 else value, high)
                    low = jnp.where(at_x == slot, pltpu.roll(value, slot, 1) if slot else value, low)
            xs_out[0, step, chunk, off:off + 16] = high.astype(BF16)
            xs_out[1, step, chunk, off:off + 16] = low.astype(BF16)
        for side in range(2):

            @pl.when(has_side[1 - side])
            def _(side=side):
                x_copy(step, chunk, side).start()

    for chunk in ORDER:
        pltpu.make_async_copy(narrow.at[0, chunk], narrow.at[0, chunk], main_recv.at[chunk]).wait()
        master[chunk] = narrow[0, chunk].astype(F32)
        publish(0, chunk)

    def back_copy(chunk, k):
        peer = lax.rem(spec + k, GROUP)
        return pltpu.make_async_remote_copy(
            src_ref=narrow.at[STEPS, chunk, pl.ds(pl.multiple_of(peer * OWN, OWN), OWN)],
            dst_ref=back.at[chunk, block],
            send_sem=back_send,
            recv_sem=back_recv.at[chunk],
            device_id=(peer, tile),
            device_id_type=MESH,
        )

    def table_of(step, chunk, yy):
        return coeff[pl.ds(pl.multiple_of((step * BLOCK + 2 * chunk + yy) * 8, 8), 8), :]

    def before_edges(step, chunk):
        if chunk == 0:
            y_copy(step, 0).wait_recv()
        if chunk == CHUNKS - 1:
            y_copy(step, 1).wait_recv()
        inner = jnp.dot(narrow[step, chunk], band[step, chunk], preferred_element_type=F32)
        for yy in range(2):
            lanes = slice(yy * LANES, (yy + 1) * LANES)
            if yy == 0:
                outer = ys_in[step, 0] if chunk == 0 else narrow[step, chunk - 1, :, LANES:]
            else:
                outer = ys_in[step, 1] if chunk == CHUNKS - 1 else narrow[step, chunk + 1, :, :LANES]
            k_outer = table_of(step, chunk, yy)[5 + yy:6 + yy]
            master[chunk, :, lanes] += inner[:, lanes] + k_outer * outer.astype(F32)

    def do_chunk(step, chunk):
        both = has_side[0] & has_side[1]

        @pl.when(both)
        def _():
            whole = xs_in.at[step, chunk]
            pltpu.make_async_copy(whole, whole, x_recv.at[step, chunk]).wait()

        @pl.when(jnp.logical_not(both))
        def _():
            one = xs_in.at[step, chunk, 0]
            pltpu.make_async_copy(one, one, x_recv.at[step, chunk]).wait()

        tables = [table_of(step, chunk, yy) for yy in range(2)]
        for off in range(0, 64, 32):
            halo_l = xs_in[step, chunk, 0, off:off + 32].astype(F32)
            halo_r = xs_in[step, chunk, 1, off:off + 32].astype(F32)
            for q in range(4):
                for yy in range(2):
                    slot = 2 * q + yy
                    at = slice(off + q * 64, off + q * 64 + 32)
                    lanes = slice(yy * LANES, (yy + 1) * LANES)
                    from_l = pltpu.roll(halo_l, LANES - slot, 1) if slot else halo_l
                    from_r = pltpu.roll(halo_r, 7 - slot, 1) if slot < 7 else halo_r
                    new = master[chunk, at, lanes] + tables[yy][7:8] * jnp.where(at_x == 0, from_l, from_r)
                    master[chunk, at, lanes] = new
                    narrow[step + 1, chunk, at, lanes] = new.astype(BF16)

        cells = narrow[step + 1, chunk]
        pre = jnp.dot(weight_in[...], cells, preferred_element_type=F32)
        hidden[...] = (pre + pre * jnp.tanh(pre)).astype(BF16)
        after = master[chunk] + jnp.dot(weight_out[...], hidden[...], preferred_element_type=F32)
        master[chunk] = after
        narrow[step + 1, chunk] = after.astype(BF16)

        @pl.when(step < STEPS - 1)
        def _():
            publish(step + 1, chunk)

        @pl.when(step == STEPS - 1)
        def _():
            pltpu.make_async_copy(narrow.at[STEPS, chunk, mine], back.at[chunk, block], back_recv.at[chunk]).start()
            for k in PEERS:
                back_copy(chunk, k).start()

    def do_step(step, carry):
        for chunk in (1, 2, 0, 3):
            before_edges(step, chunk)
        for chunk in ORDER:
            do_chunk(step, chunk)
        return carry

    lax.fori_loop(0, STEPS, do_step, 0)

    def drain(ref, sem):
        pltpu.make_async_copy(ref, ref, sem).wait()

    @pl.when(has_side[0])
    def _():
        beyond_copy.wait_send()

    for side in range(2):

        @pl.when(has_side[1 - side])
        def _(side=side):
            drain(xs_out.at[side], x_send.at[side])

    drain(flux_out.at[pl.ds(0, GROUP - 1)], flux_send)
    drain(sent.at[pl.ds(0, (GROUP - 1) * CHUNKS)], main_send)
    drain(ys_in, y_send)
    for chunk in ORDER:
        drain(back.at[chunk], back_recv.at[chunk])
    drain(sent.at[pl.ds(0, (GROUP - 1) * CHUNKS)], back_send)


def turn_back(back, out, part_in, wide, part_out, load, store):
    loads = [pltpu.make_async_copy(back.at[chunk], part_in.at[chunk], load.at[chunk]) for chunk in range(CHUNKS)]
    for copy in loads:
        copy.start()
    for chunk in range(CHUNKS):
        loads[chunk].wait()

        def widen(of, carry, chunk=chunk):
            for yy in range(2):
                y = of * BLOCK + 2 * chunk + yy
                wide[pl.ds(pl.multiple_of(y * OWN, OWN), OWN), :] = part_in[
                    chunk, of, :, yy * LANES:(yy + 1) * LANES
                ].astype(F32)
            return carry

        lax.fori_loop(0, GROUP, widen, 0, unroll=4)
    stores = []
    for part in range(4):
        for i in range(4):
            own = part * 4 + i
            part_out[own] = wide[pl.ds(own, LANES, stride=OWN), :].T.reshape(16, 8, LANES)
        span = pl.ds(4 * part, 4)
        stores.append(pltpu.make_async_copy(part_out.at[span], out.at[span], store.at[part]))
        stores[-1].start()
    for copy in stores:
        copy.wait()


def per_device(tracers, fluxes, weight_in, weight_out):
    dma = pltpu.SemaphoreType.DMA
    hbm = pl.BlockSpec(memory_space=pltpu.HBM)
    back = pl.pallas_call(
        transport,
        out_shape=jax.ShapeDtypeStruct((CHUNKS, GROUP, OWN, PAIR), BF16),
        in_specs=[hbm] * 4,
        out_specs=hbm,
        scratch_shapes=[
            pltpu.VMEM(tracers.shape, F32),
            pltpu.VMEM(fluxes.shape, F32),
            pltpu.VMEM((HID, SPEC), BF16),
            pltpu.VMEM((SPEC, HID), BF16),
            pltpu.VMEM((LANES * OWN, LANES), F32),
            pltpu.VMEM((LANES // 2, OWN, PAIR), BF16),
            pltpu.VMEM((GROUP, BLOCK, LANES), BF16),
            pltpu.VMEM((GROUP, BLOCK, LANES), BF16),
            pltpu.VMEM((STEPS, BLOCK, LANES), F32),
            pltpu.VMEM((STEPS, BLOCK, LANES), F32),
            pltpu.VMEM((STEPS + 1, CHUNKS, SPEC, PAIR), BF16),
            pltpu.VMEM((CHUNKS, SPEC, PAIR), F32),
            pltpu.VMEM((STEPS * 64, LANES), F32),
            pltpu.VMEM((STEPS, CHUNKS, PAIR, PAIR), BF16),
            pltpu.VMEM((2, STEPS, CHUNKS, 64, LANES), BF16),
            pltpu.VMEM((STEPS, CHUNKS, 2, 64, LANES), BF16),
            pltpu.VMEM((STEPS, 2, SPEC, LANES), BF16),
            pltpu.VMEM((HID, PAIR), BF16),
            dma((7,)), dma(()), dma(()), dma((2,)), dma(()), dma((CHUNKS,)),
            dma((2,)), dma((STEPS, CHUNKS)), dma(()), dma((STEPS, 2)), dma(()), dma((CHUNKS,)),
        ],
        compiler_params=pltpu.CompilerParams(collective_id=0, has_side_effects=True, vmem_limit_bytes=67043328),
        name="transport",
    )(tracers, fluxes, weight_in, weight_out)
    return pl.pallas_call(
        turn_back,
        out_shape=jax.ShapeDtypeStruct(tracers.shape, F32),
        in_specs=[hbm],
        out_specs=hbm,
        scratch_shapes=[
            pltpu.VMEM((CHUNKS, GROUP, OWN, PAIR), BF16),
            pltpu.VMEM((LANES * OWN, LANES), F32),
            pltpu.VMEM(tracers.shape, F32),
            dma((CHUNKS,)), dma((4,)),
        ],
        compiler_params=pltpu.CompilerParams(vmem_limit_bytes=67043328),
        name="turn_back",
    )(back)


def solution(mesh):
    placed = (P("species", None, "tile", None), P(None, None, "species", "tile", None), P(), P())
    return jax.shard_map(
        per_device,
        mesh=mesh,
        in_specs=placed,
        out_specs=P("species", None, "tile", None),
        check_vma=False,
    )
```

```python
import jax
import jax.numpy as jnp
from jax import lax
from jax.experimental import pallas as pl
from jax.experimental.pallas import tpu as pltpu
from jax.sharding import PartitionSpec as P

STEPS = 4
GROUP = 16
TILES = 16
LANES = 128
PAIR = 2 * LANES
SPEC = 256
HID = 512
OWN = 16
BLOCK = 8
CHUNKS = 4
EDGE_ROWS = 128
ORDER = (0, 3, 1, 2)
PEERS = (8, 4, 12, 2, 9, 5, 13, 3, 10, 6, 14, 1, 11, 7, 15)
F32 = jnp.float32
BF16 = jnp.bfloat16
MESH = pl.DeviceIdType.MESH


def block_of(device):
    return (device // 2) % 2 * 8 + device // 4 * 2 + device % 2


def transport(
    tracers_hbm, fluxes_hbm, weight_in_hbm, weight_out_hbm, back,
    tracers, fluxes, weight_in, weight_out, turned, sent, flux_out, flux_in, beyond_out, beyond_in,
    narrow, master, coeff, band, xs_out, xs_in, ys_in, hidden,
    load, flux_send, flux_recv, beyond_sem, main_send, main_recv,
    x_send, x_recv, y_send, y_recv, back_send, back_recv,
):
    spec = lax.axis_index("species")
    tile = lax.axis_index("tile")
    block = block_of(spec)
    half = block // 8
    across = spec + 2 - 4 * half
    left_device = (across, jnp.where(half == 1, tile, tile - 1))
    right_device = (across, jnp.where(half == 0, tile, tile + 1))
    part = block % 8

    def along_y(rows_at):
        return (rows_at // 2 * 4 + half * 2 + rows_at % 2, tile)

    upper = along_y(lax.rem(part + 1, 8))
    lower = along_y(lax.rem(part + 7, 8))
    at_start = (tile == 0) & (half == 0)
    at_end = (tile == TILES - 1) & (half == 1)
    has_side = (jnp.logical_not(at_start), jnp.logical_not(at_end))
    side_devices = (left_device, right_device)
    lane = lax.broadcasted_iota(jnp.int32, (1, LANES), 1)
    at_x = lane % 4
    at_p = lane // 4 % 2
    at_z = lane // 8

    def halves(even, odd):
        return (
            jnp.where(at_p == 0, even, pltpu.roll(odd, 4, 1)),
            jnp.where(at_p == 0, pltpu.roll(even, LANES - 4, 1), odd),
        )

    mine = pl.ds(pl.multiple_of(spec * OWN, OWN), OWN)

    loads = [
        pltpu.make_async_copy(fluxes_hbm, fluxes, load.at[0]),
        pltpu.make_async_copy(weight_in_hbm, weight_in, load.at[1]),
        pltpu.make_async_copy(weight_out_hbm, weight_out, load.at[2]),
    ]
    quarters = [
        pltpu.make_async_copy(tracers_hbm.at[pl.ds(4 * i, 4)], tracers.at[pl.ds(4 * i, 4)], load.at[3 + i])
        for i in range(4)
    ]
    loads = loads[:1] + quarters + loads[1:]
    for copy in loads:
        copy.start()

    barrier = pltpu.get_barrier_semaphore()

    def greet(k, carry):
        pl.semaphore_signal(
            barrier, inc=1, device_id=(lax.rem(spec + k, GROUP), tile), device_id_type=MESH
        )
        return carry

    lax.fori_loop(1, GROUP, greet, 0)
    for side in range(2):

        @pl.when(has_side[side])
        def _(side=side):
            pl.semaphore_signal(barrier, inc=1, device_id=side_devices[side], device_id_type=MESH)

        @pl.when(jnp.logical_not(has_side[side]))
        def _(side=side):
            xs_in[:, :, side] = jnp.zeros((STEPS, CHUNKS, EDGE_ROWS, LANES), BF16)
            if side == 1:
                beyond_in[...] = jnp.zeros((STEPS, BLOCK, LANES), F32)

    loads[0].wait()
    rows = []
    for step in range(STEPS):
        flux_y = fluxes[step, 1, 0]
        rows += [fluxes[step, 0, 0], flux_y, fluxes[step, 2, 0], pltpu.roll(flux_y, LANES - 1, 1)]
    turned[:LANES] = jnp.concatenate(rows, 0).T
    pairs = halves(turned[pl.ds(0, LANES // 2, stride=2), :], turned[pl.ds(1, LANES // 2, stride=2), :])
    for to in range(GROUP):
        flux_out[to] = pairs[to // 8][to % 8 * BLOCK:(to % 8 + 1) * BLOCK].astype(BF16)

    for part in range(4):
        quarters[part].wait()
        for i in range(4):
            own = part * 4 + i
            turned[pl.ds(own, LANES, stride=OWN), :] = tracers[own].reshape(LANES, LANES).T

    def narrowed(to, carry):
        for chunk in range(CHUNKS):
            for yy in range(2):
                at = pl.multiple_of((to * 16 + chunk * 4 + yy * 2) * OWN, 2 * OWN)
                both = halves(turned[pl.ds(at, OWN), :], turned[pl.ds(at + OWN, OWN), :])
                for of in range(2):
                    sent[of * 8 + to, chunk, :, yy * LANES:(yy + 1) * LANES] = both[of].astype(BF16)
        return carry

    lax.fori_loop(0, 8, narrowed, 0)

    pl.semaphore_wait(barrier, GROUP - 1 + has_side[0].astype(jnp.int32) + has_side[1].astype(jnp.int32))

    def flux_copy(k):
        peer = lax.rem(spec + k, GROUP)
        return pltpu.make_async_remote_copy(
            src_ref=flux_out.at[block_of(peer)],
            dst_ref=flux_in.at[spec],
            send_sem=flux_send,
            recv_sem=flux_recv,
            device_id=(peer, tile),
            device_id_type=MESH,
        )

    def main_copy(chunk, k):
        peer = lax.rem(spec + k, GROUP)
        return pltpu.make_async_remote_copy(
            src_ref=sent.at[block_of(peer), chunk],
            dst_ref=narrow.at[0, chunk, mine],
            send_sem=main_send,
            recv_sem=main_recv.at[chunk],
            device_id=(peer, tile),
            device_id_type=MESH,
        )

    pltpu.make_async_copy(flux_out.at[block], flux_in.at[spec], flux_recv).start()

    for k in PEERS:
        flux_copy(k).start()
    for chunk in ORDER:
        pltpu.make_async_copy(
            sent.at[block, chunk], narrow.at[0, chunk, mine], main_recv.at[chunk]
        ).start()
        for k in PEERS:
            main_copy(chunk, k).start()

    loads[5].wait()
    loads[6].wait()
    weight_in[...] = weight_in[...] * jnp.asarray(0.5, BF16)
    weight_out[...] = weight_out[...] * jnp.asarray(0.5, BF16)

    pltpu.make_async_copy(flux_in, flux_in, flux_recv).wait()
    beyond_copy = pltpu.make_async_remote_copy(
        src_ref=beyond_out,
        dst_ref=beyond_in,
        send_sem=beyond_sem.at[0],
        recv_sem=beyond_sem.at[1],
        device_id=left_device,
        device_id_type=MESH,
    )
    pieces = [flux_in[level].astype(F32) for level in range(16)]

    def field_of(step, field):
        value = jnp.zeros((BLOCK, LANES), F32)
        for level in range(16):
            shift = (level * 8 - (step * 4 + field) * 8) % LANES
            value = jnp.where(at_z == level, pltpu.roll(pieces[level], shift, 1) if shift else pieces[level], value)
        return value

    for step in range(STEPS):
        beyond_out[step] = jnp.where((at_x == 0) & at_start, 0.0, field_of(step, 0))

    @pl.when(has_side[0])
    def _():
        beyond_copy.start()

    others = [[field_of(step, field) for field in (1, 2, 3)] for step in range(STEPS)]

    @pl.when(has_side[1])
    def _():
        beyond_copy.wait_recv()

    for step in range(STEPS):
        flux_x = beyond_out[step]
        flux_y, flux_z, flux_y_up = others[step]
        beyond = jnp.where(at_end, 0.0, pltpu.roll(beyond_in[step], 3, 1))
        flux_z = jnp.where(at_z == 0, 0.0, flux_z)
        flux_x_up = jnp.where(at_x == 3, beyond, pltpu.roll(flux_x, LANES - 1, 1))
        flux_z_up = pltpu.roll(flux_z, LANES - 8, 1)
        lows = [jnp.minimum(f, 0.0) for f in (flux_x, flux_y, flux_z)]
        highs = [jnp.maximum(f, 0.0) for f in (flux_x_up, flux_y_up, flux_z_up)]
        west, east = jnp.maximum(flux_x, 0.0), -jnp.minimum(flux_x_up, 0.0)
        terms = [
            (lows[0] - highs[0]) + (lows[1] - highs[1]) + (lows[2] - highs[2]),
            jnp.where(at_x == 0, 0.0, west),
            jnp.where(at_x == 3, 0.0, east),
            jnp.maximum(flux_z, 0.0),
            -jnp.minimum(flux_z_up, 0.0),
            jnp.maximum(flux_y, 0.0),
            -jnp.minimum(flux_y_up, 0.0),
            jnp.where(at_x == 0, west, jnp.where(at_x == 3, east, 0.0)),
        ]
        for which, term in enumerate(terms):
            coeff[pl.ds(step * 64 + which, BLOCK, stride=8), :] = term

    def bands(part, carry):
        at = pl.multiple_of((part % 8) * 16, 16)
        step = part // 8
        away = lax.broadcasted_iota(jnp.int32, (16, LANES), 1) - (
            lax.broadcasted_iota(jnp.int32, (16, LANES), 0) + at
        )
        parity = lax.broadcasted_iota(jnp.int32, (16, LANES), 1) // 4 % 2
        masks = [away == d for d in (0, 1, -1, 8, -8)]
        masks += [(away == 4) & (parity == 1), (away == -4) & (parity == 0)]
        crossing = [(away == 4) & (parity == 1), (away == -4) & (parity == 0)]
        for chunk in range(CHUNKS):
            for yy in range(2):
                table = coeff[pl.ds(pl.multiple_of((step * BLOCK + 2 * chunk + yy) * 8, 8), 8), :]
                value = jnp.zeros((16, LANES), F32)
                for i in range(7):
                    value = jnp.where(masks[i], table[i:i + 1], value)
                cross = jnp.where(crossing[yy], table[6:7] if yy == 0 else table[5:6], 0.0)
                lanes = slice(yy * LANES, (yy + 1) * LANES)
                band[step, chunk, pl.ds(yy * LANES + at, 16), lanes] = value.astype(BF16)
                band[step, chunk, pl.ds((1 - yy) * LANES + at, 16), lanes] = cross.astype(BF16)
        return carry

    lax.fori_loop(0, 8 * STEPS, bands, 0)

    def x_copy(step, chunk, side):
        return pltpu.make_async_remote_copy(
            src_ref=xs_out.at[side, step, chunk],
            dst_ref=xs_in.at[step, chunk, side],
            send_sem=x_send.at[side],
            recv_sem=x_recv.at[step, chunk],
            device_id=side_devices[1 - side],
            device_id_type=MESH,
        )

    def y_copy(step, side):
        return pltpu.make_async_remote_copy(
            src_ref=narrow.at[step, CHUNKS - 1 if side == 0 else 0, :, pl.ds(LANES if side == 0 else 0, LANES)],
            dst_ref=ys_in.at[step, side],
            send_sem=y_send,
            recv_sem=y_recv.at[step, side],
            device_id=upper if side == 0 else lower,
            device_id_type=MESH,
        )

    def publish(step, chunk):
        if chunk == 0:
            y_copy(step, 1).start()
        if chunk == CHUNKS - 1:
            y_copy(step, 0).start()
        for off in range(0, EDGE_ROWS, 16):
            high = jnp.zeros((16, LANES), F32)
            low = jnp.zeros((16, LANES), F32)
            for q in range(2):
                for yy in range(2):
                    slot = 2 * q + yy
                    at = q * EDGE_ROWS + off
                    value = master[chunk, at:at + 16, yy * LANES:(yy + 1) * LANES]
                    high = jnp.where(at_x == slot, pltpu.roll(value, (slot - 3) % LANES, 1) if slot < 3 else value, high)
                    low = jnp.where(at_x == slot, pltpu.roll(value, slot, 1) if slot else value, low)
            xs_out[0, step, chunk, off:off + 16] = high.astype(BF16)
            xs_out[1, step, chunk, off:off + 16] = low.astype(BF16)
        for side in range(2):

            @pl.when(has_side[1 - side])
            def _(side=side):
                x_copy(step, chunk, side).start()

    for chunk in ORDER:
        pltpu.make_async_copy(narrow.at[0, chunk], narrow.at[0, chunk], main_recv.at[chunk]).wait()
        master[chunk] = narrow[0, chunk].astype(F32)
        publish(0, chunk)

    def back_copy(chunk, k):
        peer = lax.rem(spec + k, GROUP)
        return pltpu.make_async_remote_copy(
            src_ref=narrow.at[STEPS, chunk, pl.ds(pl.multiple_of(peer * OWN, OWN), OWN)],
            dst_ref=back.at[chunk, block],
            send_sem=back_send,
            recv_sem=back_recv.at[chunk],
            device_id=(peer, tile),
            device_id_type=MESH,
        )

    def table_of(step, chunk, yy):
        return coeff[pl.ds(pl.multiple_of((step * BLOCK + 2 * chunk + yy) * 8, 8), 8), :]

    def outer_of(step, chunk, yy, rows):
        factor = jnp.where(at_p == yy, table_of(step, chunk, yy)[5 + yy:6 + yy], 0.0)
        return factor * pltpu.roll(rows.astype(F32), LANES - 4 if yy == 0 else 4, 1)

    def before_edges(step, chunk):
        inner = jnp.dot(narrow[step, chunk], band[step, chunk], preferred_element_type=F32)
        for yy in range(2):
            lanes = slice(yy * LANES, (yy + 1) * LANES)
            new = master[chunk, :, lanes] + inner[:, lanes]
            if yy == 0 and chunk > 0:
                new += outer_of(step, chunk, yy, narrow[step, chunk - 1, :, LANES:])
            if yy == 1 and chunk < CHUNKS - 1:
                new += outer_of(step, chunk, yy, narrow[step, chunk + 1, :, :LANES])
            master[chunk, :, lanes] = new

    def do_chunk(step, chunk):
        both = has_side[0] & has_side[1]

        @pl.when(both)
        def _():
            whole = xs_in.at[step, chunk]
            pltpu.make_async_copy(whole, whole, x_recv.at[step, chunk]).wait()

        @pl.when(jnp.logical_not(both))
        def _():
            one = xs_in.at[step, chunk, 0]
            pltpu.make_async_copy(one, one, x_recv.at[step, chunk]).wait()

        if chunk == 0:
            y_copy(step, 0).wait_recv()
        if chunk == CHUNKS - 1:
            y_copy(step, 1).wait_recv()

        for off in range(0, EDGE_ROWS, 32):
            halo_l = xs_in[step, chunk, 0, off:off + 32].astype(F32)
            halo_r = xs_in[step, chunk, 1, off:off + 32].astype(F32)
            for q in range(2):
                for yy in range(2):
                    slot = 2 * q + yy
                    at = slice(off + q * EDGE_ROWS, off + q * EDGE_ROWS + 32)
                    lanes = slice(yy * LANES, (yy + 1) * LANES)
                    from_l = pltpu.roll(halo_l, LANES - slot, 1) if slot else halo_l
                    from_r = pltpu.roll(halo_r, 3 - slot, 1) if slot < 3 else halo_r
                    factor = table_of(step, chunk, yy)[7:8]
                    new = master[chunk, at, lanes] + factor * jnp.where(at_x == 0, from_l, from_r)
                    if yy == 0 and chunk == 0:
                        new += outer_of(step, chunk, yy, ys_in[step, 0, at])
                    if yy == 1 and chunk == CHUNKS - 1:
                        new += outer_of(step, chunk, yy, ys_in[step, 1, at])
                    master[chunk, at, lanes] = new
                    narrow[step + 1, chunk, at, lanes] = new.astype(BF16)

        cells = narrow[step + 1, chunk]
        pre = jnp.dot(weight_in[...], cells, preferred_element_type=F32)
        hidden[...] = (pre + pre * jnp.tanh(pre)).astype(BF16)
        after = master[chunk] + jnp.dot(weight_out[...], hidden[...], preferred_element_type=F32)
        master[chunk] = after
        narrow[step + 1, chunk] = after.astype(BF16)

        @pl.when(step < STEPS - 1)
        def _():
            publish(step + 1, chunk)

        @pl.when(step == STEPS - 1)
        def _():
            pltpu.make_async_copy(narrow.at[STEPS, chunk, mine], back.at[chunk, block], back_recv.at[chunk]).start()
            for k in PEERS:
                back_copy(chunk, k).start()

    def do_step(step, carry):
        for chunk in ORDER:
            before_edges(step, chunk)
        for chunk in ORDER:
            do_chunk(step, chunk)
        return carry

    lax.fori_loop(0, STEPS, do_step, 0)

    def drain(ref, sem):
        pltpu.make_async_copy(ref, ref, sem).wait()

    @pl.when(has_side[0])
    def _():
        beyond_copy.wait_send()

    for side in range(2):

        @pl.when(has_side[1 - side])
        def _(side=side):
            drain(xs_out.at[side], x_send.at[side])

    drain(flux_out.at[pl.ds(0, GROUP - 1)], flux_send)
    drain(sent.at[pl.ds(0, GROUP - 1)], main_send)
    drain(ys_in, y_send)
    for chunk in ORDER:
        drain(back.at[chunk], back_recv.at[chunk])
    drain(sent.at[pl.ds(0, GROUP - 1)], back_send)


def turn_back(back, out, part_in, wide, part_out, load, store):
    loads = [pltpu.make_async_copy(back.at[chunk], part_in.at[chunk], load.at[chunk]) for chunk in range(CHUNKS)]
    for copy in loads:
        copy.start()
    at_p = lax.broadcasted_iota(jnp.int32, (1, LANES), 1) // 4 % 2
    for chunk in range(CHUNKS):
        loads[chunk].wait()

        def widen(of, carry, chunk=chunk):
            for yy in range(2):
                lanes = slice(yy * LANES, (yy + 1) * LANES)
                first = part_in[chunk, of, :, lanes].astype(F32)
                second = part_in[chunk, of + 8, :, lanes].astype(F32)
                at = pl.multiple_of((of * 16 + chunk * 4 + yy * 2) * OWN, 2 * OWN)
                wide[pl.ds(at, OWN), :] = jnp.where(at_p == 0, first, pltpu.roll(second, 4, 1))
                wide[pl.ds(at + OWN, OWN), :] = jnp.where(at_p == 0, pltpu.roll(first, LANES - 4, 1), second)
            return carry

        lax.fori_loop(0, 8, widen, 0, unroll=2)
    stores = []
    for part in range(4):
        for i in range(4):
            own = part * 4 + i
            part_out[own] = wide[pl.ds(own, LANES, stride=OWN), :].T.reshape(16, 8, LANES)
        span = pl.ds(4 * part, 4)
        stores.append(pltpu.make_async_copy(part_out.at[span], out.at[span], store.at[part]))
        stores[-1].start()
    for copy in stores:
        copy.wait()


def per_device(tracers, fluxes, weight_in, weight_out):
    dma = pltpu.SemaphoreType.DMA
    hbm = pl.BlockSpec(memory_space=pltpu.HBM)
    back = pl.pallas_call(
        transport,
        out_shape=jax.ShapeDtypeStruct((CHUNKS, GROUP, OWN, PAIR), BF16),
        in_specs=[hbm] * 4,
        out_specs=hbm,
        scratch_shapes=[
            pltpu.VMEM(tracers.shape, F32),
            pltpu.VMEM(fluxes.shape, F32),
            pltpu.VMEM((HID, SPEC), BF16),
            pltpu.VMEM((SPEC, HID), BF16),
            pltpu.VMEM((LANES * OWN, LANES), F32),
            pltpu.VMEM((GROUP, CHUNKS, OWN, PAIR), BF16),
            pltpu.VMEM((GROUP, BLOCK, LANES), BF16),
            pltpu.VMEM((GROUP, BLOCK, LANES), BF16),
            pltpu.VMEM((STEPS, BLOCK, LANES), F32),
            pltpu.VMEM((STEPS, BLOCK, LANES), F32),
            pltpu.VMEM((STEPS + 1, CHUNKS, SPEC, PAIR), BF16),
            pltpu.VMEM((CHUNKS, SPEC, PAIR), F32),
            pltpu.VMEM((STEPS * 64, LANES), F32),
            pltpu.VMEM((STEPS, CHUNKS, PAIR, PAIR), BF16),
            pltpu.VMEM((2, STEPS, CHUNKS, EDGE_ROWS, LANES), BF16),
            pltpu.VMEM((STEPS, CHUNKS, 2, EDGE_ROWS, LANES), BF16),
            pltpu.VMEM((STEPS, 2, SPEC, LANES), BF16),
            pltpu.VMEM((HID, PAIR), BF16),
            dma((7,)), dma(()), dma(()), dma((2,)), dma(()), dma((CHUNKS,)),
            dma((2,)), dma((STEPS, CHUNKS)), dma(()), dma((STEPS, 2)), dma(()), dma((CHUNKS,)),
        ],
        compiler_params=pltpu.CompilerParams(collective_id=0, has_side_effects=True, vmem_limit_bytes=67043328),
        name="transport",
    )(tracers, fluxes, weight_in, weight_out)
    return pl.pallas_call(
        turn_back,
        out_shape=jax.ShapeDtypeStruct(tracers.shape, F32),
        in_specs=[hbm],
        out_specs=hbm,
        scratch_shapes=[
            pltpu.VMEM((CHUNKS, GROUP, OWN, PAIR), BF16),
            pltpu.VMEM((LANES * OWN, LANES), F32),
            pltpu.VMEM(tracers.shape, F32),
            dma((CHUNKS,)), dma((4,)),
        ],
        compiler_params=pltpu.CompilerParams(vmem_limit_bytes=67043328),
        name="turn_back",
    )(back)


def solution(mesh):
    placed = (P("species", None, "tile", None), P(None, None, "species", "tile", None), P(), P())
    return jax.shard_map(
        per_device,
        mesh=mesh,
        in_specs=placed,
        out_specs=P("species", None, "tile", None),
        check_vma=False,
    )
```

```python
import jax
import jax.numpy as jnp
from jax import lax
from jax.experimental import pallas as pl
from jax.experimental.pallas import tpu as pltpu
from jax.sharding import PartitionSpec as P

STEPS = 4
GROUP = 16
TILES = 16
LANES = 128
PAIR = 2 * LANES
SPEC = 256
HID = 512
OWN = 16
BLOCK = 8
CHUNKS = 4
EDGE_ROWS = 128
ORDER = (0, 3, 1, 2)
PEERS = (8, 4, 12, 2, 9, 5, 13, 3, 10, 6, 14, 1, 11, 7, 15)
F32 = jnp.float32
BF16 = jnp.bfloat16
MESH = pl.DeviceIdType.MESH


def block_of(device):
    return (device // 2) % 2 * 8 + device // 4 * 2 + device % 2


def transport(
    tracers_hbm, fluxes_hbm, weight_in_hbm, weight_out_hbm, back,
    tracers, fluxes, weight_in, weight_out, turned, sent, flux_out, flux_in, beyond_out, beyond_in,
    narrow, master, coeff, band, xs_out, xs_in, ys_in, hidden,
    load, flux_send, flux_recv, beyond_sem, main_send, main_recv,
    x_send, x_recv, y_send, y_recv, back_send, back_recv,
):
    spec = lax.axis_index("species")
    tile = lax.axis_index("tile")
    block = block_of(spec)
    half = block // 8
    across = spec + 2 - 4 * half
    left_device = (across, jnp.where(half == 1, tile, tile - 1))
    right_device = (across, jnp.where(half == 0, tile, tile + 1))
    part = block % 8

    def along_y(rows_at):
        return (rows_at // 2 * 4 + half * 2 + rows_at % 2, tile)

    upper = along_y(lax.rem(part + 1, 8))
    lower = along_y(lax.rem(part + 7, 8))
    at_start = (tile == 0) & (half == 0)
    at_end = (tile == TILES - 1) & (half == 1)
    has_side = (jnp.logical_not(at_start), jnp.logical_not(at_end))
    side_devices = (left_device, right_device)
    lane = lax.broadcasted_iota(jnp.int32, (1, LANES), 1)
    at_x = lane % 4
    at_p = lane // 4 % 2
    at_z = lane // 8

    def halves(even, odd):
        return (
            jnp.where(at_p == 0, even, pltpu.roll(odd, 4, 1)),
            jnp.where(at_p == 0, pltpu.roll(even, LANES - 4, 1), odd),
        )

    mine = pl.ds(pl.multiple_of(spec * OWN, OWN), OWN)

    loads = [
        pltpu.make_async_copy(fluxes_hbm, fluxes, load.at[0]),
        pltpu.make_async_copy(weight_in_hbm, weight_in, load.at[1]),
        pltpu.make_async_copy(weight_out_hbm, weight_out, load.at[2]),
    ]
    quarters = [
        pltpu.make_async_copy(tracers_hbm.at[pl.ds(4 * i, 4)], tracers.at[pl.ds(4 * i, 4)], load.at[3 + i])
        for i in range(4)
    ]
    loads = loads[:1] + quarters + loads[1:]
    for copy in loads:
        copy.start()

    barrier = pltpu.get_barrier_semaphore()

    def greet(k, carry):
        pl.semaphore_signal(
            barrier, inc=1, device_id=(lax.rem(spec + k, GROUP), tile), device_id_type=MESH
        )
        return carry

    lax.fori_loop(1, GROUP, greet, 0)
    for side in range(2):

        @pl.when(has_side[side])
        def _(side=side):
            pl.semaphore_signal(barrier, inc=1, device_id=side_devices[side], device_id_type=MESH)

        @pl.when(jnp.logical_not(has_side[side]))
        def _(side=side):
            xs_in[:, :, side] = jnp.zeros((STEPS, CHUNKS, EDGE_ROWS, LANES), BF16)
            if side == 1:
                beyond_in[...] = jnp.zeros((STEPS, BLOCK, LANES), F32)

    loads[0].wait()
    rows = []
    for step in range(STEPS):
        flux_y = fluxes[step, 1, 0]
        rows += [fluxes[step, 0, 0], flux_y, fluxes[step, 2, 0], pltpu.roll(flux_y, LANES - 1, 1)]
    turned[:LANES] = jnp.concatenate(rows, 0).T
    pairs = halves(turned[pl.ds(0, LANES // 2, stride=2), :], turned[pl.ds(1, LANES // 2, stride=2), :])
    for to in range(GROUP):
        flux_out[to] = pairs[to // 8][to % 8 * BLOCK:(to % 8 + 1) * BLOCK].astype(BF16)

    for part in range(4):
        quarters[part].wait()
        for i in range(4):
            own = part * 4 + i
            turned[pl.ds(own, LANES, stride=OWN), :] = tracers[own].reshape(LANES, LANES).T

    def narrowed(to, carry):
        for chunk in range(CHUNKS):
            for yy in range(2):
                at = pl.multiple_of((to * 16 + chunk * 4 + yy * 2) * OWN, 2 * OWN)
                both = halves(turned[pl.ds(at, OWN), :], turned[pl.ds(at + OWN, OWN), :])
                for of in range(2):
                    sent[of * 8 + to, chunk, :, yy * LANES:(yy + 1) * LANES] = both[of].astype(BF16)
        return carry

    lax.fori_loop(0, 8, narrowed, 0)

    pl.semaphore_wait(barrier, GROUP - 1 + has_side[0].astype(jnp.int32) + has_side[1].astype(jnp.int32))

    def flux_copy(k):
        peer = lax.rem(spec + k, GROUP)
        return pltpu.make_async_remote_copy(
            src_ref=flux_out.at[block_of(peer)],
            dst_ref=flux_in.at[spec],
            send_sem=flux_send,
            recv_sem=flux_recv,
            device_id=(peer, tile),
            device_id_type=MESH,
        )

    def main_copy(chunk, k):
        peer = lax.rem(spec + k, GROUP)
        return pltpu.make_async_remote_copy(
            src_ref=sent.at[block_of(peer), chunk],
            dst_ref=narrow.at[0, chunk, mine],
            send_sem=main_send,
            recv_sem=main_recv.at[chunk],
            device_id=(peer, tile),
            device_id_type=MESH,
        )

    pltpu.make_async_copy(flux_out.at[block], flux_in.at[spec], flux_recv).start()

    for k in PEERS:
        flux_copy(k).start()
    for chunk in ORDER:
        pltpu.make_async_copy(
            sent.at[block, chunk], narrow.at[0, chunk, mine], main_recv.at[chunk]
        ).start()
        for k in PEERS:
            main_copy(chunk, k).start()

    loads[5].wait()
    loads[6].wait()
    weight_in[...] = weight_in[...] * jnp.asarray(0.5, BF16)
    weight_out[...] = weight_out[...] * jnp.asarray(0.5, BF16)

    pltpu.make_async_copy(flux_in, flux_in, flux_recv).wait()
    beyond_copy = pltpu.make_async_remote_copy(
        src_ref=beyond_out,
        dst_ref=beyond_in,
        send_sem=beyond_sem.at[0],
        recv_sem=beyond_sem.at[1],
        device_id=left_device,
        device_id_type=MESH,
    )
    pieces = [flux_in[level].astype(F32) for level in range(16)]

    def field_of(step, field):
        value = jnp.zeros((BLOCK, LANES), F32)
        for level in range(16):
            shift = (level * 8 - (step * 4 + field) * 8) % LANES
            value = jnp.where(at_z == level, pltpu.roll(pieces[level], shift, 1) if shift else pieces[level], value)
        return value

    for step in range(STEPS):
        beyond_out[step] = jnp.where((at_x == 0) & at_start, 0.0, field_of(step, 0))

    @pl.when(has_side[0])
    def _():
        beyond_copy.start()

    others = [[field_of(step, field) for field in (1, 2, 3)] for step in range(STEPS)]

    @pl.when(has_side[1])
    def _():
        beyond_copy.wait_recv()

    for step in range(STEPS):
        flux_x = beyond_out[step]
        flux_y, flux_z, flux_y_up = others[step]
        beyond = jnp.where(at_end, 0.0, pltpu.roll(beyond_in[step], 3, 1))
        flux_z = jnp.where(at_z == 0, 0.0, flux_z)
        flux_x_up = jnp.where(at_x == 3, beyond, pltpu.roll(flux_x, LANES - 1, 1))
        flux_z_up = pltpu.roll(flux_z, LANES - 8, 1)
        lows = [jnp.minimum(f, 0.0) for f in (flux_x, flux_y, flux_z)]
        highs = [jnp.maximum(f, 0.0) for f in (flux_x_up, flux_y_up, flux_z_up)]
        west, east = jnp.maximum(flux_x, 0.0), -jnp.minimum(flux_x_up, 0.0)
        terms = [
            (lows[0] - highs[0]) + (lows[1] - highs[1]) + (lows[2] - highs[2]),
            jnp.where(at_x == 0, 0.0, west),
            jnp.where(at_x == 3, 0.0, east),
            jnp.maximum(flux_z, 0.0),
            -jnp.minimum(flux_z_up, 0.0),
            jnp.maximum(flux_y, 0.0),
            -jnp.minimum(flux_y_up, 0.0),
            jnp.where(at_x == 0, west, jnp.where(at_x == 3, east, 0.0)),
        ]
        for which, term in enumerate(terms):
            coeff[pl.ds(step * 64 + which, BLOCK, stride=8), :] = term

    def bands(part, carry):
        at = pl.multiple_of((part % 8) * 16, 16)
        step = part // 8
        away = lax.broadcasted_iota(jnp.int32, (16, LANES), 1) - (
            lax.broadcasted_iota(jnp.int32, (16, LANES), 0) + at
        )
        parity = lax.broadcasted_iota(jnp.int32, (16, LANES), 1) // 4 % 2
        masks = [away == d for d in (0, 1, -1, 8, -8)]
        masks += [(away == 4) & (parity == 1), (away == -4) & (parity == 0)]
        crossing = [(away == 4) & (parity == 1), (away == -4) & (parity == 0)]
        for chunk in range(CHUNKS):
            for yy in range(2):
                table = coeff[pl.ds(pl.multiple_of((step * BLOCK + 2 * chunk + yy) * 8, 8), 8), :]
                value = jnp.zeros((16, LANES), F32)
                for i in range(7):
                    value = jnp.where(masks[i], table[i:i + 1], value)
                cross = jnp.where(crossing[yy], table[6:7] if yy == 0 else table[5:6], 0.0)
                lanes = slice(yy * LANES, (yy + 1) * LANES)
                band[step, chunk, pl.ds(yy * LANES + at, 16), lanes] = value.astype(BF16)
                band[step, chunk, pl.ds((1 - yy) * LANES + at, 16), lanes] = cross.astype(BF16)
        return carry

    lax.fori_loop(0, 8 * STEPS, bands, 0)

    def x_copy(step, chunk, side):
        return pltpu.make_async_remote_copy(
            src_ref=xs_out.at[side, step, chunk],
            dst_ref=xs_in.at[step, chunk, side],
            send_sem=x_send.at[side],
            recv_sem=x_recv.at[step, chunk],
            device_id=side_devices[1 - side],
            device_id_type=MESH,
        )

    def y_copy(step, side):
        return pltpu.make_async_remote_copy(
            src_ref=narrow.at[step, CHUNKS - 1 if side == 0 else 0, :, pl.ds(LANES if side == 0 else 0, LANES)],
            dst_ref=ys_in.at[step, side],
            send_sem=y_send,
            recv_sem=y_recv.at[step, side],
            device_id=upper if side == 0 else lower,
            device_id_type=MESH,
        )

    def publish(step, chunk):
        if chunk == 0:
            y_copy(step, 1).start()
        if chunk == CHUNKS - 1:
            y_copy(step, 0).start()
        for off in range(0, EDGE_ROWS, 32):
            high = low = None
            for q in range(2):
                for yy in range(2):
                    slot = 2 * q + yy
                    at = q * EDGE_ROWS + off
                    value = narrow[step, chunk, at:at + 32, yy * LANES:(yy + 1) * LANES]
                    up = pltpu.roll(value, (slot - 3) % LANES, 1) if slot < 3 else value
                    down = pltpu.roll(value, slot, 1) if slot else value
                    high = up if slot == 0 else jnp.where(at_x == slot, up, high)
                    low = down if slot == 0 else jnp.where(at_x == slot, down, low)
            xs_out[0, step, chunk, off:off + 32] = high
            xs_out[1, step, chunk, off:off + 32] = low
        for side in range(2):

            @pl.when(has_side[1 - side])
            def _(side=side):
                x_copy(step, chunk, side).start()

    for chunk in ORDER:
        pltpu.make_async_copy(narrow.at[0, chunk], narrow.at[0, chunk], main_recv.at[chunk]).wait()
        master[chunk] = narrow[0, chunk].astype(F32)
        publish(0, chunk)

    def back_copy(chunk, k):
        peer = lax.rem(spec + k, GROUP)
        return pltpu.make_async_remote_copy(
            src_ref=narrow.at[STEPS, chunk, pl.ds(pl.multiple_of(peer * OWN, OWN), OWN)],
            dst_ref=back.at[chunk, block],
            send_sem=back_send,
            recv_sem=back_recv.at[chunk],
            device_id=(peer, tile),
            device_id_type=MESH,
        )

    def table_of(step, chunk, yy):
        return coeff[pl.ds(pl.multiple_of((step * BLOCK + 2 * chunk + yy) * 8, 8), 8), :]

    def outer_of(step, chunk, yy, rows):
        factor = jnp.where(at_p == yy, table_of(step, chunk, yy)[5 + yy:6 + yy], 0.0)
        return factor * pltpu.roll(rows.astype(F32), LANES - 4 if yy == 0 else 4, 1)

    def before_edges(step, chunk):
        inner = jnp.dot(narrow[step, chunk], band[step, chunk], preferred_element_type=F32)
        for yy in range(2):
            lanes = slice(yy * LANES, (yy + 1) * LANES)
            new = master[chunk, :, lanes] + inner[:, lanes]
            if yy == 0 and chunk > 0:
                new += outer_of(step, chunk, yy, narrow[step, chunk - 1, :, LANES:])
            if yy == 1 and chunk < CHUNKS - 1:
                new += outer_of(step, chunk, yy, narrow[step, chunk + 1, :, :LANES])
            master[chunk, :, lanes] = new

    def do_chunk(step, chunk):
        both = has_side[0] & has_side[1]

        @pl.when(both)
        def _():
            whole = xs_in.at[step, chunk]
            pltpu.make_async_copy(whole, whole, x_recv.at[step, chunk]).wait()

        @pl.when(jnp.logical_not(both))
        def _():
            one = xs_in.at[step, chunk, 0]
            pltpu.make_async_copy(one, one, x_recv.at[step, chunk]).wait()

        if chunk == 0:
            y_copy(step, 0).wait_recv()
        if chunk == CHUNKS - 1:
            y_copy(step, 1).wait_recv()

        for off in range(0, EDGE_ROWS, 32):
            halo_l = xs_in[step, chunk, 0, off:off + 32]
            halo_r = xs_in[step, chunk, 1, off:off + 32]
            for q in range(2):
                for yy in range(2):
                    slot = 2 * q + yy
                    at = slice(off + q * EDGE_ROWS, off + q * EDGE_ROWS + 32)
                    lanes = slice(yy * LANES, (yy + 1) * LANES)
                    from_l = pltpu.roll(halo_l, LANES - slot, 1) if slot else halo_l
                    from_r = pltpu.roll(halo_r, 3 - slot, 1) if slot < 3 else halo_r
                    factor = table_of(step, chunk, yy)[7:8]
                    new = master[chunk, at, lanes] + factor * jnp.where(at_x == 0, from_l, from_r).astype(F32)
                    if yy == 0 and chunk == 0:
                        new += outer_of(step, chunk, yy, ys_in[step, 0, at])
                    if yy == 1 and chunk == CHUNKS - 1:
                        new += outer_of(step, chunk, yy, ys_in[step, 1, at])
                    master[chunk, at, lanes] = new
                    narrow[step + 1, chunk, at, lanes] = new.astype(BF16)

        cells = narrow[step + 1, chunk]
        pre = jnp.dot(weight_in[...], cells, preferred_element_type=F32)
        hidden[...] = (pre + pre * jnp.tanh(pre)).astype(BF16)
        after = master[chunk] + jnp.dot(weight_out[...], hidden[...], preferred_element_type=F32)
        master[chunk] = after
        narrow[step + 1, chunk] = after.astype(BF16)

        @pl.when(step < STEPS - 1)
        def _():
            publish(step + 1, chunk)

        @pl.when(step == STEPS - 1)
        def _():
            pltpu.make_async_copy(narrow.at[STEPS, chunk, mine], back.at[chunk, block], back_recv.at[chunk]).start()
            for k in PEERS:
                back_copy(chunk, k).start()

    def do_step(step, carry):
        for chunk in ORDER:
            before_edges(step, chunk)
        for chunk in ORDER:
            do_chunk(step, chunk)
        return carry

    lax.fori_loop(0, STEPS, do_step, 0)

    def drain(ref, sem):
        pltpu.make_async_copy(ref, ref, sem).wait()

    @pl.when(has_side[0])
    def _():
        beyond_copy.wait_send()

    for side in range(2):

        @pl.when(has_side[1 - side])
        def _(side=side):
            drain(xs_out.at[side], x_send.at[side])

    drain(flux_out.at[pl.ds(0, GROUP - 1)], flux_send)
    drain(sent.at[pl.ds(0, GROUP - 1)], main_send)
    drain(ys_in, y_send)
    for chunk in ORDER:
        drain(back.at[chunk], back_recv.at[chunk])
    drain(sent.at[pl.ds(0, GROUP - 1)], back_send)


def turn_back(back, out, part_in, wide, part_out, load, store):
    loads = [pltpu.make_async_copy(back.at[chunk], part_in.at[chunk], load.at[chunk]) for chunk in range(CHUNKS)]
    for copy in loads:
        copy.start()
    at_p = lax.broadcasted_iota(jnp.int32, (1, LANES), 1) // 4 % 2
    for chunk in range(CHUNKS):
        loads[chunk].wait()

        def widen(of, carry, chunk=chunk):
            for yy in range(2):
                lanes = slice(yy * LANES, (yy + 1) * LANES)
                first = part_in[chunk, of, :, lanes].astype(F32)
                second = part_in[chunk, of + 8, :, lanes].astype(F32)
                at = pl.multiple_of((of * 16 + chunk * 4 + yy * 2) * OWN, 2 * OWN)
                wide[pl.ds(at, OWN), :] = jnp.where(at_p == 0, first, pltpu.roll(second, 4, 1))
                wide[pl.ds(at + OWN, OWN), :] = jnp.where(at_p == 0, pltpu.roll(first, LANES - 4, 1), second)
            return carry

        lax.fori_loop(0, 8, widen, 0, unroll=8)
    stores = []
    for part in range(4):
        for i in range(4):
            own = part * 4 + i
            part_out[own] = wide[pl.ds(own, LANES, stride=OWN), :].T.reshape(16, 8, LANES)
        span = pl.ds(4 * part, 4)
        stores.append(pltpu.make_async_copy(part_out.at[span], out.at[span], store.at[part]))
        stores[-1].start()
    for copy in stores:
        copy.wait()


def per_device(tracers, fluxes, weight_in, weight_out):
    dma = pltpu.SemaphoreType.DMA
    hbm = pl.BlockSpec(memory_space=pltpu.HBM)
    back = pl.pallas_call(
        transport,
        out_shape=jax.ShapeDtypeStruct((CHUNKS, GROUP, OWN, PAIR), BF16),
        in_specs=[hbm] * 4,
        out_specs=hbm,
        scratch_shapes=[
            pltpu.VMEM(tracers.shape, F32),
            pltpu.VMEM(fluxes.shape, F32),
            pltpu.VMEM((HID, SPEC), BF16),
            pltpu.VMEM((SPEC, HID), BF16),
            pltpu.VMEM((LANES * OWN, LANES), F32),
            pltpu.VMEM((GROUP, CHUNKS, OWN, PAIR), BF16),
            pltpu.VMEM((GROUP, BLOCK, LANES), BF16),
            pltpu.VMEM((GROUP, BLOCK, LANES), BF16),
            pltpu.VMEM((STEPS, BLOCK, LANES), F32),
            pltpu.VMEM((STEPS, BLOCK, LANES), F32),
            pltpu.VMEM((STEPS + 1, CHUNKS, SPEC, PAIR), BF16),
            pltpu.VMEM((CHUNKS, SPEC, PAIR), F32),
            pltpu.VMEM((STEPS * 64, LANES), F32),
            pltpu.VMEM((STEPS, CHUNKS, PAIR, PAIR), BF16),
            pltpu.VMEM((2, STEPS, CHUNKS, EDGE_ROWS, LANES), BF16),
            pltpu.VMEM((STEPS, CHUNKS, 2, EDGE_ROWS, LANES), BF16),
            pltpu.VMEM((STEPS, 2, SPEC, LANES), BF16),
            pltpu.VMEM((HID, PAIR), BF16),
            dma((7,)), dma(()), dma(()), dma((2,)), dma(()), dma((CHUNKS,)),
            dma((2,)), dma((STEPS, CHUNKS)), dma(()), dma((STEPS, 2)), dma(()), dma((CHUNKS,)),
        ],
        compiler_params=pltpu.CompilerParams(collective_id=0, has_side_effects=True, vmem_limit_bytes=67043328),
        name="transport",
    )(tracers, fluxes, weight_in, weight_out)
    return pl.pallas_call(
        turn_back,
        out_shape=jax.ShapeDtypeStruct(tracers.shape, F32),
        in_specs=[hbm],
        out_specs=hbm,
        scratch_shapes=[
            pltpu.VMEM((CHUNKS, GROUP, OWN, PAIR), BF16),
            pltpu.VMEM((LANES * OWN, LANES), F32),
            pltpu.VMEM(tracers.shape, F32),
            dma((CHUNKS,)), dma((4,)),
        ],
        compiler_params=pltpu.CompilerParams(vmem_limit_bytes=67043328),
        name="turn_back",
    )(back)


def solution(mesh):
    placed = (P("species", None, "tile", None), P(None, None, "species", "tile", None), P(), P())
    return jax.shard_map(
        per_device,
        mesh=mesh,
        in_specs=placed,
        out_specs=P("species", None, "tile", None),
        check_vma=False,
    )
```

```python
import jax
import jax.numpy as jnp
from jax import lax
from jax.experimental import pallas as pl
from jax.experimental.pallas import tpu as pltpu
from jax.sharding import PartitionSpec as P

STEPS = 4
GROUP = 16
TILES = 16
LANES = 128
PAIR = 2 * LANES
SPEC = 256
HID = 512
OWN = 16
BLOCK = 8
CHUNKS = 4
EDGE_ROWS = 128
ORDER = (0, 3, 1, 2)
PLACE = (0, 2, 3, 1)
PEERS = (8, 4, 12, 2, 9, 5, 13, 3, 10, 6, 14, 1, 11, 7, 15)
F32 = jnp.float32
BF16 = jnp.bfloat16
MESH = pl.DeviceIdType.MESH


def block_of(device):
    return (device // 2) % 2 * 8 + device // 4 * 2 + device % 2


def transport(
    tracers_hbm, fluxes_hbm, weight_in_hbm, weight_out_hbm, back,
    tracers, fluxes, weight_in, weight_out, turned, sent, flux_out, flux_in, beyond_out, beyond_in,
    narrow, master, coeff, band, xs_out, xs_in, ys_out, ys_in, hidden,
    load, flux_send, flux_recv, beyond_sem, main_send, main_recv,
    x_send, x_recv, y_send, y_recv, back_send, back_recv,
):
    spec = lax.axis_index("species")
    tile = lax.axis_index("tile")
    block = block_of(spec)
    half = block // 8
    across = spec + 2 - 4 * half
    left_device = (across, jnp.where(half == 1, tile, tile - 1))
    right_device = (across, jnp.where(half == 0, tile, tile + 1))
    part = block % 8

    def along_y(rows_at):
        return (rows_at // 2 * 4 + half * 2 + rows_at % 2, tile)

    upper = along_y(lax.rem(part + 1, 8))
    lower = along_y(lax.rem(part + 7, 8))
    at_start = (tile == 0) & (half == 0)
    at_end = (tile == TILES - 1) & (half == 1)
    has_side = (jnp.logical_not(at_start), jnp.logical_not(at_end))
    side_devices = (left_device, right_device)
    lane = lax.broadcasted_iota(jnp.int32, (1, LANES), 1)
    at_x = lane % 4
    at_p = lane // 4 % 2
    at_z = lane // 8

    def halves(even, odd):
        return (
            jnp.where(at_p == 0, even, pltpu.roll(odd, 4, 1)),
            jnp.where(at_p == 0, pltpu.roll(even, LANES - 4, 1), odd),
        )

    mine = pl.ds(pl.multiple_of(spec * OWN, OWN), OWN)

    loads = [
        pltpu.make_async_copy(fluxes_hbm, fluxes, load.at[0]),
        pltpu.make_async_copy(weight_in_hbm, weight_in, load.at[1]),
        pltpu.make_async_copy(weight_out_hbm, weight_out, load.at[2]),
    ]
    quarters = [
        pltpu.make_async_copy(tracers_hbm.at[pl.ds(4 * i, 4)], tracers.at[pl.ds(4 * i, 4)], load.at[3 + i])
        for i in range(4)
    ]
    loads = loads[:1] + quarters + loads[1:]
    for copy in loads:
        copy.start()

    barrier = pltpu.get_barrier_semaphore()

    def greet(k, carry):
        pl.semaphore_signal(
            barrier, inc=1, device_id=(lax.rem(spec + k, GROUP), tile), device_id_type=MESH
        )
        return carry

    lax.fori_loop(1, GROUP, greet, 0)
    for side in range(2):

        @pl.when(has_side[side])
        def _(side=side):
            pl.semaphore_signal(barrier, inc=1, device_id=side_devices[side], device_id_type=MESH)

        @pl.when(jnp.logical_not(has_side[side]))
        def _(side=side):
            xs_in[:, :, side] = jnp.zeros((STEPS, CHUNKS, EDGE_ROWS, LANES), BF16)
            if side == 1:
                beyond_in[...] = jnp.zeros((STEPS, BLOCK, LANES), F32)

    loads[0].wait()
    rows = []
    for step in range(STEPS):
        flux_y = fluxes[step, 1, 0]
        rows += [fluxes[step, 0, 0], flux_y, fluxes[step, 2, 0], pltpu.roll(flux_y, LANES - 1, 1)]
    turned[:LANES] = jnp.concatenate(rows, 0).T
    pairs = halves(turned[pl.ds(0, LANES // 2, stride=2), :], turned[pl.ds(1, LANES // 2, stride=2), :])
    for to in range(GROUP):
        flux_out[to] = pairs[to // 8][to % 8 * BLOCK:(to % 8 + 1) * BLOCK].astype(BF16)

    for part in range(4):
        quarters[part].wait()
        for i in range(4):
            own = part * 4 + i
            turned[pl.ds(own, LANES, stride=OWN), :] = tracers[own].reshape(LANES, LANES).T

    def narrowed(to, carry):
        for chunk in range(CHUNKS):
            for yy in range(2):
                at = pl.multiple_of((to * 16 + chunk * 4 + yy * 2) * OWN, 2 * OWN)
                both = halves(turned[pl.ds(at, OWN), :], turned[pl.ds(at + OWN, OWN), :])
                for of in range(2):
                    sent[of * 8 + to, PLACE[chunk], :, yy * LANES:(yy + 1) * LANES] = both[of].astype(BF16)
        return carry

    lax.fori_loop(0, 8, narrowed, 0)

    pl.semaphore_wait(barrier, GROUP - 1 + has_side[0].astype(jnp.int32) + has_side[1].astype(jnp.int32))

    def flux_copy(k):
        peer = lax.rem(spec + k, GROUP)
        return pltpu.make_async_remote_copy(
            src_ref=flux_out.at[block_of(peer)],
            dst_ref=flux_in.at[spec],
            send_sem=flux_send,
            recv_sem=flux_recv,
            device_id=(peer, tile),
            device_id_type=MESH,
        )

    def main_copy(pair, k):
        peer = lax.rem(spec + k, GROUP)
        return pltpu.make_async_remote_copy(
            src_ref=sent.at[block_of(peer), pl.ds(2 * pair, 2)],
            dst_ref=narrow.at[0, pl.ds(2 * pair, 2), mine],
            send_sem=main_send,
            recv_sem=main_recv.at[pair],
            device_id=(peer, tile),
            device_id_type=MESH,
        )

    pltpu.make_async_copy(flux_out.at[block], flux_in.at[spec], flux_recv).start()

    for k in PEERS:
        flux_copy(k).start()
    for pair in range(2):
        span = pl.ds(2 * pair, 2)
        pltpu.make_async_copy(sent.at[block, span], narrow.at[0, span, mine], main_recv.at[pair]).start()
        for k in PEERS:
            main_copy(pair, k).start()

    loads[5].wait()
    loads[6].wait()
    weight_in[...] = weight_in[...] * jnp.asarray(0.5, BF16)
    weight_out[...] = weight_out[...] * jnp.asarray(0.5, BF16)

    pltpu.make_async_copy(flux_in, flux_in, flux_recv).wait()
    beyond_copy = pltpu.make_async_remote_copy(
        src_ref=beyond_out,
        dst_ref=beyond_in,
        send_sem=beyond_sem.at[0],
        recv_sem=beyond_sem.at[1],
        device_id=left_device,
        device_id_type=MESH,
    )
    pieces = [flux_in[level].astype(F32) for level in range(16)]

    def field_of(step, field):
        value = jnp.zeros((BLOCK, LANES), F32)
        for level in range(16):
            shift = (level * 8 - (step * 4 + field) * 8) % LANES
            value = jnp.where(at_z == level, pltpu.roll(pieces[level], shift, 1) if shift else pieces[level], value)
        return value

    for step in range(STEPS):
        beyond_out[step] = jnp.where((at_x == 0) & at_start, 0.0, field_of(step, 0))

    @pl.when(has_side[0])
    def _():
        beyond_copy.start()

    others = [[field_of(step, field) for field in (1, 2, 3)] for step in range(STEPS)]

    def x_copy(step, chunk, side):
        return pltpu.make_async_remote_copy(
            src_ref=xs_out.at[side, step, chunk],
            dst_ref=xs_in.at[step, chunk, side],
            send_sem=x_send.at[side],
            recv_sem=x_recv.at[step, chunk],
            device_id=side_devices[1 - side],
            device_id_type=MESH,
        )

    def y_copy(step, side):
        return pltpu.make_async_remote_copy(
            src_ref=ys_out.at[step, side],
            dst_ref=ys_in.at[step, side],
            send_sem=y_send,
            recv_sem=y_recv.at[step, side],
            device_id=upper if side == 0 else lower,
            device_id_type=MESH,
        )

    def publish_y(step, side):
        chunk, at = (CHUNKS - 1, LANES) if side == 0 else (0, 0)
        first = narrow[step, PLACE[chunk], :EDGE_ROWS, at:at + LANES]
        second = narrow[step, PLACE[chunk], EDGE_ROWS:, at:at + LANES]
        ys_out[step, side] = jnp.where(at_p == 1 - side, first, pltpu.roll(second, 4 if side else LANES - 4, 1))
        y_copy(step, side).start()

    def publish(step, chunk):
        if chunk == 0:
            publish_y(step, 1)
        if chunk == CHUNKS - 1:
            publish_y(step, 0)
        for off in range(0, EDGE_ROWS, 32):
            high = low = None
            for q in range(2):
                for yy in range(2):
                    slot = 2 * q + yy
                    at = q * EDGE_ROWS + off
                    value = narrow[step, PLACE[chunk], at:at + 32, yy * LANES:(yy + 1) * LANES]
                    up = pltpu.roll(value, (slot - 3) % LANES, 1) if slot < 3 else value
                    down = pltpu.roll(value, slot, 1) if slot else value
                    high = up if slot == 0 else jnp.where(at_x == slot, up, high)
                    low = down if slot == 0 else jnp.where(at_x == slot, down, low)
            xs_out[0, step, chunk, off:off + 32] = high
            xs_out[1, step, chunk, off:off + 32] = low
        for side in range(2):

            @pl.when(has_side[1 - side])
            def _(side=side):
                x_copy(step, chunk, side).start()

    for chunk in ORDER:
        if PLACE[chunk] % 2 == 0:
            whole = narrow.at[0, pl.ds(PLACE[chunk], 2)]
            pltpu.make_async_copy(whole, whole, main_recv.at[PLACE[chunk] // 2]).wait()
        master[chunk] = narrow[0, PLACE[chunk]].astype(F32)
        publish(0, chunk)

    @pl.when(has_side[1])
    def _():
        beyond_copy.wait_recv()

    for step in range(STEPS):
        flux_x = beyond_out[step]
        flux_y, flux_z, flux_y_up = others[step]
        beyond = jnp.where(at_end, 0.0, pltpu.roll(beyond_in[step], 3, 1))
        flux_z = jnp.where(at_z == 0, 0.0, flux_z)
        flux_x_up = jnp.where(at_x == 3, beyond, pltpu.roll(flux_x, LANES - 1, 1))
        flux_z_up = pltpu.roll(flux_z, LANES - 8, 1)
        lows = [jnp.minimum(f, 0.0) for f in (flux_x, flux_y, flux_z)]
        highs = [jnp.maximum(f, 0.0) for f in (flux_x_up, flux_y_up, flux_z_up)]
        west, east = jnp.maximum(flux_x, 0.0), -jnp.minimum(flux_x_up, 0.0)
        terms = [
            (lows[0] - highs[0]) + (lows[1] - highs[1]) + (lows[2] - highs[2]),
            jnp.where(at_x == 0, 0.0, west),
            jnp.where(at_x == 3, 0.0, east),
            jnp.maximum(flux_z, 0.0),
            -jnp.minimum(flux_z_up, 0.0),
            jnp.maximum(flux_y, 0.0),
            -jnp.minimum(flux_y_up, 0.0),
            jnp.where(at_x == 0, west, jnp.where(at_x == 3, east, 0.0)),
        ]
        for which, term in enumerate(terms):
            coeff[pl.ds(step * 64 + which, BLOCK, stride=8), :] = term

    def bands(part, carry):
        at = pl.multiple_of((part % 8) * 16, 16)
        step = part // 8
        away = lax.broadcasted_iota(jnp.int32, (16, LANES), 1) - (
            lax.broadcasted_iota(jnp.int32, (16, LANES), 0) + at
        )
        parity = lax.broadcasted_iota(jnp.int32, (16, LANES), 1) // 4 % 2
        masks = [away == d for d in (0, 1, -1, 8, -8)]
        masks += [(away == 4) & (parity == 1), (away == -4) & (parity == 0)]
        crossing = [(away == 4) & (parity == 1), (away == -4) & (parity == 0)]
        for chunk in range(CHUNKS):
            for yy in range(2):
                table = coeff[pl.ds(pl.multiple_of((step * BLOCK + 2 * chunk + yy) * 8, 8), 8), :]
                value = jnp.zeros((16, LANES), F32)
                for i in range(7):
                    value = jnp.where(masks[i], table[i:i + 1], value)
                cross = jnp.where(crossing[yy], table[6:7] if yy == 0 else table[5:6], 0.0)
                lanes = slice(yy * LANES, (yy + 1) * LANES)
                band[step, chunk, pl.ds(yy * LANES + at, 16), lanes] = value.astype(BF16)
                band[step, chunk, pl.ds((1 - yy) * LANES + at, 16), lanes] = cross.astype(BF16)
        return carry

    lax.fori_loop(0, 8 * STEPS, bands, 0)

    def back_copy(chunk, k):
        peer = lax.rem(spec + k, GROUP)
        return pltpu.make_async_remote_copy(
            src_ref=narrow.at[STEPS, PLACE[chunk], pl.ds(pl.multiple_of(peer * OWN, OWN), OWN)],
            dst_ref=back.at[chunk, block],
            send_sem=back_send,
            recv_sem=back_recv.at[chunk],
            device_id=(peer, tile),
            device_id_type=MESH,
        )

    def table_of(step, chunk, yy):
        return coeff[pl.ds(pl.multiple_of((step * BLOCK + 2 * chunk + yy) * 8, 8), 8), :]

    def outer_of(step, chunk, yy, rows, in_place=False):
        factor = jnp.where(at_p == yy, table_of(step, chunk, yy)[5 + yy:6 + yy], 0.0)
        if not in_place:
            rows = pltpu.roll(rows, LANES - 4 if yy == 0 else 4, 1)
        return factor * rows.astype(F32)

    def before_edges(step, chunk):
        inner = jnp.dot(narrow[step, PLACE[chunk]], band[step, chunk], preferred_element_type=F32)
        for yy in range(2):
            lanes = slice(yy * LANES, (yy + 1) * LANES)
            new = master[chunk, :, lanes] + inner[:, lanes]
            if yy == 0 and chunk > 0:
                new += outer_of(step, chunk, yy, narrow[step, PLACE[chunk - 1], :, LANES:])
            if yy == 1 and chunk < CHUNKS - 1:
                new += outer_of(step, chunk, yy, narrow[step, PLACE[chunk + 1], :, :LANES])
            master[chunk, :, lanes] = new

    def do_chunk(step, chunk):
        both = has_side[0] & has_side[1]

        @pl.when(both)
        def _():
            whole = xs_in.at[step, chunk]
            pltpu.make_async_copy(whole, whole, x_recv.at[step, chunk]).wait()

        @pl.when(jnp.logical_not(both))
        def _():
            one = xs_in.at[step, chunk, 0]
            pltpu.make_async_copy(one, one, x_recv.at[step, chunk]).wait()

        if chunk == 0:
            y_copy(step, 0).wait_recv()
        if chunk == CHUNKS - 1:
            y_copy(step, 1).wait_recv()

        for off in range(0, EDGE_ROWS, 32):
            halo_l = xs_in[step, chunk, 0, off:off + 32]
            halo_r = xs_in[step, chunk, 1, off:off + 32]
            for q in range(2):
                for yy in range(2):
                    slot = 2 * q + yy
                    at = slice(off + q * EDGE_ROWS, off + q * EDGE_ROWS + 32)
                    lanes = slice(yy * LANES, (yy + 1) * LANES)
                    from_l = pltpu.roll(halo_l, LANES - slot, 1) if slot else halo_l
                    from_r = pltpu.roll(halo_r, 3 - slot, 1) if slot < 3 else halo_r
                    factor = table_of(step, chunk, yy)[7:8]
                    new = master[chunk, at, lanes] + factor * jnp.where(at_x == 0, from_l, from_r).astype(F32)
                    if yy == 0 and chunk == 0:
                        new += outer_of(step, chunk, yy, ys_in[step, 0, off:off + 32], q == 1)
                    if yy == 1 and chunk == CHUNKS - 1:
                        new += outer_of(step, chunk, yy, ys_in[step, 1, off:off + 32], q == 1)
                    master[chunk, at, lanes] = new
                    narrow[step + 1, PLACE[chunk], at, lanes] = new.astype(BF16)

        cells = narrow[step + 1, PLACE[chunk]]
        pre = jnp.dot(weight_in[...], cells, preferred_element_type=F32)
        hidden[...] = (pre + pre * jnp.tanh(pre)).astype(BF16)
        after = master[chunk] + jnp.dot(weight_out[...], hidden[...], preferred_element_type=F32)
        master[chunk] = after
        narrow[step + 1, PLACE[chunk]] = after.astype(BF16)

        @pl.when(step < STEPS - 1)
        def _():
            publish(step + 1, chunk)

        @pl.when(step == STEPS - 1)
        def _():
            pltpu.make_async_copy(narrow.at[STEPS, PLACE[chunk], mine], back.at[chunk, block], back_recv.at[chunk]).start()
            for k in PEERS:
                back_copy(chunk, k).start()

    def do_step(step, carry):
        for chunk in ORDER:
            before_edges(step, chunk)
        for chunk in ORDER:
            do_chunk(step, chunk)
        return carry

    lax.fori_loop(0, STEPS, do_step, 0)

    def drain(ref, sem):
        pltpu.make_async_copy(ref, ref, sem).wait()

    @pl.when(has_side[0])
    def _():
        beyond_copy.wait_send()

    for side in range(2):

        @pl.when(has_side[1 - side])
        def _(side=side):
            drain(xs_out.at[side], x_send.at[side])

    drain(flux_out.at[pl.ds(0, GROUP - 1)], flux_send)
    drain(sent.at[pl.ds(0, GROUP - 1)], main_send)
    drain(ys_in, y_send)
    for chunk in ORDER:
        drain(back.at[chunk], back_recv.at[chunk])
    drain(sent.at[pl.ds(0, GROUP - 1)], back_send)


def turn_back(back, out, part_in, wide, part_out, load, store):
    loads = [pltpu.make_async_copy(back.at[chunk], part_in.at[chunk], load.at[chunk]) for chunk in range(CHUNKS)]
    for copy in loads:
        copy.start()
    at_p = lax.broadcasted_iota(jnp.int32, (1, LANES), 1) // 4 % 2
    for chunk in range(CHUNKS):
        loads[chunk].wait()

        def widen(of, carry, chunk=chunk):
            for yy in range(2):
                lanes = slice(yy * LANES, (yy + 1) * LANES)
                first = part_in[chunk, of, :, lanes].astype(F32)
                second = part_in[chunk, of + 8, :, lanes].astype(F32)
                at = pl.multiple_of((of * 16 + chunk * 4 + yy * 2) * OWN, 2 * OWN)
                wide[pl.ds(at, OWN), :] = jnp.where(at_p == 0, first, pltpu.roll(second, 4, 1))
                wide[pl.ds(at + OWN, OWN), :] = jnp.where(at_p == 0, pltpu.roll(first, LANES - 4, 1), second)
            return carry

        lax.fori_loop(0, 8, widen, 0, unroll=8)
    stores = []
    for part in range(4):
        for i in range(4):
            own = part * 4 + i
            part_out[own] = wide[pl.ds(own, LANES, stride=OWN), :].T.reshape(16, 8, LANES)
        span = pl.ds(4 * part, 4)
        stores.append(pltpu.make_async_copy(part_out.at[span], out.at[span], store.at[part]))
        stores[-1].start()
    for copy in stores:
        copy.wait()


def per_device(tracers, fluxes, weight_in, weight_out):
    dma = pltpu.SemaphoreType.DMA
    hbm = pl.BlockSpec(memory_space=pltpu.HBM)
    back = pl.pallas_call(
        transport,
        out_shape=jax.ShapeDtypeStruct((CHUNKS, GROUP, OWN, PAIR), BF16),
        in_specs=[hbm] * 4,
        out_specs=hbm,
        scratch_shapes=[
            pltpu.VMEM(tracers.shape, F32),
            pltpu.VMEM(fluxes.shape, F32),
            pltpu.VMEM((HID, SPEC), BF16),
            pltpu.VMEM((SPEC, HID), BF16),
            pltpu.VMEM((LANES * OWN, LANES), F32),
            pltpu.VMEM((GROUP, CHUNKS, OWN, PAIR), BF16),
            pltpu.VMEM((GROUP, BLOCK, LANES), BF16),
            pltpu.VMEM((GROUP, BLOCK, LANES), BF16),
            pltpu.VMEM((STEPS, BLOCK, LANES), F32),
            pltpu.VMEM((STEPS, BLOCK, LANES), F32),
            pltpu.VMEM((STEPS + 1, CHUNKS, SPEC, PAIR), BF16),
            pltpu.VMEM((CHUNKS, SPEC, PAIR), F32),
            pltpu.VMEM((STEPS * 64, LANES), F32),
            pltpu.VMEM((STEPS, CHUNKS, PAIR, PAIR), BF16),
            pltpu.VMEM((2, STEPS, CHUNKS, EDGE_ROWS, LANES), BF16),
            pltpu.VMEM((STEPS, CHUNKS, 2, EDGE_ROWS, LANES), BF16),
            pltpu.VMEM((STEPS, 2, EDGE_ROWS, LANES), BF16),
            pltpu.VMEM((STEPS, 2, EDGE_ROWS, LANES), BF16),
            pltpu.VMEM((HID, PAIR), BF16),
            dma((7,)), dma(()), dma(()), dma((2,)), dma(()), dma((CHUNKS,)),
            dma((2,)), dma((STEPS, CHUNKS)), dma(()), dma((STEPS, 2)), dma(()), dma((CHUNKS,)),
        ],
        compiler_params=pltpu.CompilerParams(collective_id=0, has_side_effects=True, vmem_limit_bytes=67043328),
        name="transport",
    )(tracers, fluxes, weight_in, weight_out)
    return pl.pallas_call(
        turn_back,
        out_shape=jax.ShapeDtypeStruct(tracers.shape, F32),
        in_specs=[hbm],
        out_specs=hbm,
        scratch_shapes=[
            pltpu.VMEM((CHUNKS, GROUP, OWN, PAIR), BF16),
            pltpu.VMEM((LANES * OWN, LANES), F32),
            pltpu.VMEM(tracers.shape, F32),
            dma((CHUNKS,)), dma((4,)),
        ],
        compiler_params=pltpu.CompilerParams(vmem_limit_bytes=67043328),
        name="turn_back",
    )(back)


def solution(mesh):
    placed = (P("species", None, "tile", None), P(None, None, "species", "tile", None), P(), P())
    return jax.shard_map(
        per_device,
        mesh=mesh,
        in_specs=placed,
        out_specs=P("species", None, "tile", None),
        check_vma=False,
    )
```

```python
import jax
import jax.numpy as jnp
from jax import lax
from jax.experimental import pallas as pl
from jax.experimental.pallas import tpu as pltpu
from jax.sharding import PartitionSpec as P

STEPS = 4
GROUP = 16
TILES = 16
LANES = 128
PAIR = 2 * LANES
SPEC = 256
HID = 512
OWN = 16
BLOCK = 8
CHUNKS = 4
EDGE_ROWS = 128
ORDER = (1, 2, 0, 3)
PLACE = (2, 0, 1, 3)
PEERS = (8, 4, 12, 2, 9, 5, 13, 3, 10, 6, 14, 1, 11, 7, 15)
F32 = jnp.float32
BF16 = jnp.bfloat16
MESH = pl.DeviceIdType.MESH


def block_of(device):
    return (device // 2) % 2 * 8 + device // 4 * 2 + device % 2


def transport(
    tracers_hbm, fluxes_hbm, weight_in_hbm, weight_out_hbm, back,
    tracers, fluxes, weight_in, weight_out, turned, sent, flux_out, flux_in, beyond_out, beyond_in,
    narrow, master, coeff, band, xs_out, xs_in, ys_out, ys_in, hidden,
    load, flux_send, flux_recv, beyond_sem, main_send, main_recv,
    x_send, x_recv, y_send, y_recv, back_send, back_recv,
):
    spec = lax.axis_index("species")
    tile = lax.axis_index("tile")
    block = block_of(spec)
    half = block // 8
    across = spec + 2 - 4 * half
    left_device = (across, jnp.where(half == 1, tile, tile - 1))
    right_device = (across, jnp.where(half == 0, tile, tile + 1))
    part = block % 8

    def along_y(rows_at):
        return (rows_at // 2 * 4 + half * 2 + rows_at % 2, tile)

    upper = along_y(lax.rem(part + 1, 8))
    lower = along_y(lax.rem(part + 7, 8))
    at_start = (tile == 0) & (half == 0)
    at_end = (tile == TILES - 1) & (half == 1)
    has_side = (jnp.logical_not(at_start), jnp.logical_not(at_end))
    side_devices = (left_device, right_device)
    lane = lax.broadcasted_iota(jnp.int32, (1, LANES), 1)
    at_x = lane % 4
    at_p = lane // 4 % 2
    at_z = lane // 8

    def halves(even, odd):
        return (
            jnp.where(at_p == 0, even, pltpu.roll(odd, 4, 1)),
            jnp.where(at_p == 0, pltpu.roll(even, LANES - 4, 1), odd),
        )

    mine = pl.ds(pl.multiple_of(spec * OWN, OWN), OWN)

    loads = [
        pltpu.make_async_copy(fluxes_hbm, fluxes, load.at[0]),
        pltpu.make_async_copy(weight_in_hbm, weight_in, load.at[1]),
        pltpu.make_async_copy(weight_out_hbm, weight_out, load.at[2]),
    ]
    quarters = [
        pltpu.make_async_copy(tracers_hbm.at[pl.ds(4 * i, 4)], tracers.at[pl.ds(4 * i, 4)], load.at[3 + i])
        for i in range(4)
    ]
    loads = loads[:1] + quarters + loads[1:]
    for copy in loads:
        copy.start()

    barrier = pltpu.get_barrier_semaphore()

    def greet(k, carry):
        pl.semaphore_signal(
            barrier, inc=1, device_id=(lax.rem(spec + k, GROUP), tile), device_id_type=MESH
        )
        return carry

    lax.fori_loop(1, GROUP, greet, 0)
    for side in range(2):

        @pl.when(has_side[side])
        def _(side=side):
            pl.semaphore_signal(barrier, inc=1, device_id=side_devices[side], device_id_type=MESH)

        @pl.when(jnp.logical_not(has_side[side]))
        def _(side=side):
            xs_in[:, :, side] = jnp.zeros((STEPS, CHUNKS, EDGE_ROWS, LANES), BF16)
            if side == 1:
                beyond_in[...] = jnp.zeros((STEPS, BLOCK, LANES), F32)

    loads[0].wait()
    rows = []
    for step in range(STEPS):
        flux_y = fluxes[step, 1, 0]
        rows += [fluxes[step, 0, 0], flux_y, fluxes[step, 2, 0], pltpu.roll(flux_y, LANES - 1, 1)]
    turned[:LANES] = jnp.concatenate(rows, 0).T
    pairs = halves(turned[pl.ds(0, LANES // 2, stride=2), :], turned[pl.ds(1, LANES // 2, stride=2), :])
    for to in range(GROUP):
        flux_out[to] = pairs[to // 8][to % 8 * BLOCK:(to % 8 + 1) * BLOCK].astype(BF16)

    for part in range(4):
        quarters[part].wait()
        for i in range(4):
            own = part * 4 + i
            turned[pl.ds(own, LANES, stride=OWN), :] = tracers[own].reshape(LANES, LANES).T

    def narrowed(to, carry):
        for chunk in range(CHUNKS):
            for yy in range(2):
                at = pl.multiple_of((to * 16 + chunk * 4 + yy * 2) * OWN, 2 * OWN)
                both = halves(turned[pl.ds(at, OWN), :], turned[pl.ds(at + OWN, OWN), :])
                for of in range(2):
                    sent[of * 8 + to, PLACE[chunk], :, yy * LANES:(yy + 1) * LANES] = both[of].astype(BF16)
        return carry

    lax.fori_loop(0, 8, narrowed, 0)

    pl.semaphore_wait(barrier, GROUP - 1 + has_side[0].astype(jnp.int32) + has_side[1].astype(jnp.int32))

    def flux_copy(k):
        peer = lax.rem(spec + k, GROUP)
        return pltpu.make_async_remote_copy(
            src_ref=flux_out.at[block_of(peer)],
            dst_ref=flux_in.at[spec],
            send_sem=flux_send,
            recv_sem=flux_recv,
            device_id=(peer, tile),
            device_id_type=MESH,
        )

    def main_copy(pair, k):
        peer = lax.rem(spec + k, GROUP)
        return pltpu.make_async_remote_copy(
            src_ref=sent.at[block_of(peer), pl.ds(2 * pair, 2)],
            dst_ref=narrow.at[0, pl.ds(2 * pair, 2), mine],
            send_sem=main_send,
            recv_sem=main_recv.at[pair],
            device_id=(peer, tile),
            device_id_type=MESH,
        )

    pltpu.make_async_copy(flux_out.at[block], flux_in.at[spec], flux_recv).start()

    for k in PEERS:
        flux_copy(k).start()
    for pair in range(2):
        span = pl.ds(2 * pair, 2)
        pltpu.make_async_copy(sent.at[block, span], narrow.at[0, span, mine], main_recv.at[pair]).start()
        for k in PEERS:
            main_copy(pair, k).start()

    loads[5].wait()
    loads[6].wait()
    weight_in[...] = weight_in[...] * jnp.asarray(0.5, BF16)
    weight_out[...] = weight_out[...] * jnp.asarray(0.5, BF16)

    pltpu.make_async_copy(flux_in, flux_in, flux_recv).wait()
    beyond_copy = pltpu.make_async_remote_copy(
        src_ref=beyond_out,
        dst_ref=beyond_in,
        send_sem=beyond_sem.at[0],
        recv_sem=beyond_sem.at[1],
        device_id=left_device,
        device_id_type=MESH,
    )
    pieces = [flux_in[level].astype(F32) for level in range(16)]

    def field_of(step, field):
        value = jnp.zeros((BLOCK, LANES), F32)
        for level in range(16):
            shift = (level * 8 - (step * 4 + field) * 8) % LANES
            value = jnp.where(at_z == level, pltpu.roll(pieces[level], shift, 1) if shift else pieces[level], value)
        return value

    for step in range(STEPS):
        beyond_out[step] = jnp.where((at_x == 0) & at_start, 0.0, field_of(step, 0))

    @pl.when(has_side[0])
    def _():
        beyond_copy.start()


    def x_copy(step, chunk, side):
        return pltpu.make_async_remote_copy(
            src_ref=xs_out.at[side, step, chunk],
            dst_ref=xs_in.at[step, chunk, side],
            send_sem=x_send.at[side],
            recv_sem=x_recv.at[step, chunk],
            device_id=side_devices[1 - side],
            device_id_type=MESH,
        )

    def y_copy(step, side):
        return pltpu.make_async_remote_copy(
            src_ref=ys_out.at[step, side],
            dst_ref=ys_in.at[step, side],
            send_sem=y_send,
            recv_sem=y_recv.at[step, side],
            device_id=upper if side == 0 else lower,
            device_id_type=MESH,
        )

    def publish_y(step, side):
        chunk, at = (CHUNKS - 1, LANES) if side == 0 else (0, 0)
        first = narrow[step, PLACE[chunk], :EDGE_ROWS, at:at + LANES]
        second = narrow[step, PLACE[chunk], EDGE_ROWS:, at:at + LANES]
        ys_out[step, side] = jnp.where(at_p == 1 - side, first, pltpu.roll(second, 4 if side else LANES - 4, 1))
        y_copy(step, side).start()

    def publish(step, chunk):
        if chunk == 0:
            publish_y(step, 1)
        if chunk == CHUNKS - 1:
            publish_y(step, 0)
        for off in range(0, EDGE_ROWS, 32):
            high = low = None
            for q in range(2):
                for yy in range(2):
                    slot = 2 * q + yy
                    at = q * EDGE_ROWS + off
                    value = narrow[step, PLACE[chunk], at:at + 32, yy * LANES:(yy + 1) * LANES]
                    up = pltpu.roll(value, (slot - 3) % LANES, 1) if slot < 3 else value
                    down = pltpu.roll(value, slot, 1) if slot else value
                    high = up if slot == 0 else jnp.where(at_x == slot, up, high)
                    low = down if slot == 0 else jnp.where(at_x == slot, down, low)
            xs_out[0, step, chunk, off:off + 32] = high
            xs_out[1, step, chunk, off:off + 32] = low
        for side in range(2):

            @pl.when(has_side[1 - side])
            def _(side=side):
                x_copy(step, chunk, side).start()

    for chunk in ORDER:
        if PLACE[chunk] % 2 == 0:
            whole = narrow.at[0, pl.ds(PLACE[chunk], 2)]
            pltpu.make_async_copy(whole, whole, main_recv.at[PLACE[chunk] // 2]).wait()
        master[chunk] = narrow[0, PLACE[chunk]].astype(F32)
        publish(0, chunk)

    others = [[field_of(step, field) for field in (1, 2, 3)] for step in range(STEPS)]

    @pl.when(has_side[1])
    def _():
        beyond_copy.wait_recv()

    for step in range(STEPS):
        flux_x = beyond_out[step]
        flux_y, flux_z, flux_y_up = others[step]
        beyond = jnp.where(at_end, 0.0, pltpu.roll(beyond_in[step], 3, 1))
        flux_z = jnp.where(at_z == 0, 0.0, flux_z)
        flux_x_up = jnp.where(at_x == 3, beyond, pltpu.roll(flux_x, LANES - 1, 1))
        flux_z_up = pltpu.roll(flux_z, LANES - 8, 1)
        lows = [jnp.minimum(f, 0.0) for f in (flux_x, flux_y, flux_z)]
        highs = [jnp.maximum(f, 0.0) for f in (flux_x_up, flux_y_up, flux_z_up)]
        west, east = jnp.maximum(flux_x, 0.0), -jnp.minimum(flux_x_up, 0.0)
        terms = [
            (lows[0] - highs[0]) + (lows[1] - highs[1]) + (lows[2] - highs[2]),
            jnp.where(at_x == 0, 0.0, west),
            jnp.where(at_x == 3, 0.0, east),
            jnp.maximum(flux_z, 0.0),
            -jnp.minimum(flux_z_up, 0.0),
            jnp.maximum(flux_y, 0.0),
            -jnp.minimum(flux_y_up, 0.0),
            jnp.where(at_x == 0, west, jnp.where(at_x == 3, east, 0.0)),
        ]
        for which, term in enumerate(terms):
            coeff[pl.ds(step * 64 + which, BLOCK, stride=8), :] = term

    def bands(part, carry):
        at = pl.multiple_of((part % 8) * 16, 16)
        step = part // 8
        away = lax.broadcasted_iota(jnp.int32, (16, LANES), 1) - (
            lax.broadcasted_iota(jnp.int32, (16, LANES), 0) + at
        )
        parity = lax.broadcasted_iota(jnp.int32, (16, LANES), 1) // 4 % 2
        masks = [away == d for d in (0, 1, -1, 8, -8)]
        masks += [(away == 4) & (parity == 1), (away == -4) & (parity == 0)]
        crossing = [(away == 4) & (parity == 1), (away == -4) & (parity == 0)]
        for chunk in range(CHUNKS):
            for yy in range(2):
                table = coeff[pl.ds(pl.multiple_of((step * BLOCK + 2 * chunk + yy) * 8, 8), 8), :]
                value = jnp.zeros((16, LANES), F32)
                for i in range(7):
                    value = jnp.where(masks[i], table[i:i + 1], value)
                cross = jnp.where(crossing[yy], table[6:7] if yy == 0 else table[5:6], 0.0)
                lanes = slice(yy * LANES, (yy + 1) * LANES)
                band[step, chunk, pl.ds(yy * LANES + at, 16), lanes] = value.astype(BF16)
                band[step, chunk, pl.ds((1 - yy) * LANES + at, 16), lanes] = cross.astype(BF16)
        return carry

    lax.fori_loop(0, 8 * STEPS, bands, 0)

    def back_copy(chunk, k):
        peer = lax.rem(spec + k, GROUP)
        return pltpu.make_async_remote_copy(
            src_ref=narrow.at[STEPS, PLACE[chunk], pl.ds(pl.multiple_of(peer * OWN, OWN), OWN)],
            dst_ref=back.at[chunk, block],
            send_sem=back_send,
            recv_sem=back_recv.at[chunk],
            device_id=(peer, tile),
            device_id_type=MESH,
        )

    def table_of(step, chunk, yy):
        return coeff[pl.ds(pl.multiple_of((step * BLOCK + 2 * chunk + yy) * 8, 8), 8), :]

    def outer_of(step, chunk, yy, rows, in_place=False):
        factor = jnp.where(at_p == yy, table_of(step, chunk, yy)[5 + yy:6 + yy], 0.0)
        if not in_place:
            rows = pltpu.roll(rows, LANES - 4 if yy == 0 else 4, 1)
        return factor * rows.astype(F32)

    def before_edges(step, chunk):
        inner = jnp.dot(narrow[step, PLACE[chunk]], band[step, chunk], preferred_element_type=F32)
        for yy in range(2):
            lanes = slice(yy * LANES, (yy + 1) * LANES)
            new = master[chunk, :, lanes] + inner[:, lanes]
            if yy == 0 and chunk > 0:
                new += outer_of(step, chunk, yy, narrow[step, PLACE[chunk - 1], :, LANES:])
            if yy == 1 and chunk < CHUNKS - 1:
                new += outer_of(step, chunk, yy, narrow[step, PLACE[chunk + 1], :, :LANES])
            master[chunk, :, lanes] = new

    def do_chunk(step, chunk):
        both = has_side[0] & has_side[1]

        @pl.when(both)
        def _():
            whole = xs_in.at[step, chunk]
            pltpu.make_async_copy(whole, whole, x_recv.at[step, chunk]).wait()

        @pl.when(jnp.logical_not(both))
        def _():
            one = xs_in.at[step, chunk, 0]
            pltpu.make_async_copy(one, one, x_recv.at[step, chunk]).wait()

        if chunk == 0:
            y_copy(step, 0).wait_recv()
        if chunk == CHUNKS - 1:
            y_copy(step, 1).wait_recv()

        for off in range(0, EDGE_ROWS, 32):
            halo_l = xs_in[step, chunk, 0, off:off + 32]
            halo_r = xs_in[step, chunk, 1, off:off + 32]
            for q in range(2):
                for yy in range(2):
                    slot = 2 * q + yy
                    at = slice(off + q * EDGE_ROWS, off + q * EDGE_ROWS + 32)
                    lanes = slice(yy * LANES, (yy + 1) * LANES)
                    from_l = pltpu.roll(halo_l, LANES - slot, 1) if slot else halo_l
                    from_r = pltpu.roll(halo_r, 3 - slot, 1) if slot < 3 else halo_r
                    factor = table_of(step, chunk, yy)[7:8]
                    new = master[chunk, at, lanes] + factor * jnp.where(at_x == 0, from_l, from_r).astype(F32)
                    if yy == 0 and chunk == 0:
                        new += outer_of(step, chunk, yy, ys_in[step, 0, off:off + 32], q == 1)
                    if yy == 1 and chunk == CHUNKS - 1:
                        new += outer_of(step, chunk, yy, ys_in[step, 1, off:off + 32], q == 1)
                    master[chunk, at, lanes] = new
                    narrow[step + 1, PLACE[chunk], at, lanes] = new.astype(BF16)

        cells = narrow[step + 1, PLACE[chunk]]
        pre = jnp.dot(weight_in[...], cells, preferred_element_type=F32)
        hidden[...] = (pre + pre * jnp.tanh(pre)).astype(BF16)
        after = master[chunk] + jnp.dot(weight_out[...], hidden[...], preferred_element_type=F32)
        master[chunk] = after
        narrow[step + 1, PLACE[chunk]] = after.astype(BF16)

        @pl.when(step < STEPS - 1)
        def _():
            publish(step + 1, chunk)

        @pl.when(step == STEPS - 1)
        def _():
            pltpu.make_async_copy(narrow.at[STEPS, PLACE[chunk], mine], back.at[chunk, block], back_recv.at[chunk]).start()
            for k in PEERS:
                back_copy(chunk, k).start()

    def do_step(step, carry):
        for chunk in ORDER:
            before_edges(step, chunk)
        for chunk in ORDER:
            do_chunk(step, chunk)
        return carry

    lax.fori_loop(0, STEPS, do_step, 0)

    def drain(ref, sem):
        pltpu.make_async_copy(ref, ref, sem).wait()

    @pl.when(has_side[0])
    def _():
        beyond_copy.wait_send()

    for side in range(2):

        @pl.when(has_side[1 - side])
        def _(side=side):
            drain(xs_out.at[side], x_send.at[side])

    drain(flux_out.at[pl.ds(0, GROUP - 1)], flux_send)
    drain(sent.at[pl.ds(0, GROUP - 1)], main_send)
    drain(ys_in, y_send)
    for chunk in ORDER:
        drain(back.at[chunk], back_recv.at[chunk])
    drain(sent.at[pl.ds(0, GROUP - 1)], back_send)


def turn_back(back, out, part_in, wide, part_out, load, store):
    loads = [pltpu.make_async_copy(back.at[chunk], part_in.at[chunk], load.at[chunk]) for chunk in range(CHUNKS)]
    for copy in loads:
        copy.start()
    at_p = lax.broadcasted_iota(jnp.int32, (1, LANES), 1) // 4 % 2
    for chunk in range(CHUNKS):
        loads[chunk].wait()

        def widen(of, carry, chunk=chunk):
            for yy in range(2):
                lanes = slice(yy * LANES, (yy + 1) * LANES)
                first = part_in[chunk, of, :, lanes].astype(F32)
                second = part_in[chunk, of + 8, :, lanes].astype(F32)
                at = pl.multiple_of((of * 16 + chunk * 4 + yy * 2) * OWN, 2 * OWN)
                wide[pl.ds(at, OWN), :] = jnp.where(at_p == 0, first, pltpu.roll(second, 4, 1))
                wide[pl.ds(at + OWN, OWN), :] = jnp.where(at_p == 0, pltpu.roll(first, LANES - 4, 1), second)
            return carry

        lax.fori_loop(0, 8, widen, 0, unroll=8)
    stores = []
    for part in range(8):
        for i in range(2):
            own = part * 2 + i
            part_out[own] = wide[pl.ds(own, LANES, stride=OWN), :].T.reshape(16, 8, LANES)
        span = pl.ds(2 * part, 2)
        stores.append(pltpu.make_async_copy(part_out.at[span], out.at[span], store.at[part]))
        stores[-1].start()
    for copy in stores:
        copy.wait()


def per_device(tracers, fluxes, weight_in, weight_out):
    dma = pltpu.SemaphoreType.DMA
    hbm = pl.BlockSpec(memory_space=pltpu.HBM)
    back = pl.pallas_call(
        transport,
        out_shape=jax.ShapeDtypeStruct((CHUNKS, GROUP, OWN, PAIR), BF16),
        in_specs=[hbm] * 4,
        out_specs=hbm,
        scratch_shapes=[
            pltpu.VMEM(tracers.shape, F32),
            pltpu.VMEM(fluxes.shape, F32),
            pltpu.VMEM((HID, SPEC), BF16),
            pltpu.VMEM((SPEC, HID), BF16),
            pltpu.VMEM((LANES * OWN, LANES), F32),
            pltpu.VMEM((GROUP, CHUNKS, OWN, PAIR), BF16),
            pltpu.VMEM((GROUP, BLOCK, LANES), BF16),
            pltpu.VMEM((GROUP, BLOCK, LANES), BF16),
            pltpu.VMEM((STEPS, BLOCK, LANES), F32),
            pltpu.VMEM((STEPS, BLOCK, LANES), F32),
            pltpu.VMEM((STEPS + 1, CHUNKS, SPEC, PAIR), BF16),
            pltpu.VMEM((CHUNKS, SPEC, PAIR), F32),
            pltpu.VMEM((STEPS * 64, LANES), F32),
            pltpu.VMEM((STEPS, CHUNKS, PAIR, PAIR), BF16),
            pltpu.VMEM((2, STEPS, CHUNKS, EDGE_ROWS, LANES), BF16),
            pltpu.VMEM((STEPS, CHUNKS, 2, EDGE_ROWS, LANES), BF16),
            pltpu.VMEM((STEPS, 2, EDGE_ROWS, LANES), BF16),
            pltpu.VMEM((STEPS, 2, EDGE_ROWS, LANES), BF16),
            pltpu.VMEM((HID, PAIR), BF16),
            dma((7,)), dma(()), dma(()), dma((2,)), dma(()), dma((CHUNKS,)),
            dma((2,)), dma((STEPS, CHUNKS)), dma(()), dma((STEPS, 2)), dma(()), dma((CHUNKS,)),
        ],
        compiler_params=pltpu.CompilerParams(collective_id=0, has_side_effects=True, vmem_limit_bytes=67043328),
        name="transport",
    )(tracers, fluxes, weight_in, weight_out)
    return pl.pallas_call(
        turn_back,
        out_shape=jax.ShapeDtypeStruct(tracers.shape, F32),
        in_specs=[hbm],
        out_specs=hbm,
        scratch_shapes=[
            pltpu.VMEM((CHUNKS, GROUP, OWN, PAIR), BF16),
            pltpu.VMEM((LANES * OWN, LANES), F32),
            pltpu.VMEM(tracers.shape, F32),
            dma((CHUNKS,)), dma((8,)),
        ],
        compiler_params=pltpu.CompilerParams(vmem_limit_bytes=67043328),
        name="turn_back",
    )(back)


def solution(mesh):
    placed = (P("species", None, "tile", None), P(None, None, "species", "tile", None), P(), P())
    return jax.shard_map(
        per_device,
        mesh=mesh,
        in_specs=placed,
        out_specs=P("species", None, "tile", None),
        check_vma=False,
    )
```
